128 devices in a mesh: grp: 8 (over x, core), seq: 16 (over y, z).
Axes of the slice: x: 4, y: 4, z: 4, core: 2. Of those that a mesh axis runs over, the one named last changes fastest.
Arguments:
- tokens: bfloat16 [32, 4, 5120], P(None, None, ('grp', 'seq')), may hold values from -90 to 90
- lengths: int32 [32], replicated, may hold values from 1 to 16384, as said below
- group_perm: int32 [32], replicated, may hold values from 0 to 31, as said below
- page_table: int32 [32, 128], replicated, may hold values from 0 to 31, as said below
- k_pool: bfloat16 [4096, 128, 1024], P(('grp', 'seq')), may hold values from -17 to 17
- v_pool: bfloat16 [4096, 128, 1024], P(('grp', 'seq')), may hold values from -7 to 7
- gain_in: float32 [5120], P(('grp', 'seq')), may hold values from 0.25 to 1.75
- qkv_weight: bfloat16 [5120, 7168], P('grp', 'seq'), may hold values from -0.15625 to 0.15625
- qkv_bias: float32 [7168], P('seq'), may hold values from -16 to 16
- o_weight: bfloat16 [5120, 5120], P('seq', 'grp'), may hold values from -0.078125 to 0.078125
- gain_mid: float32 [5120], P(('grp', 'seq')), may hold values from 0.25 to 1.75
- gate_weight: bfloat16 [5120, 13824], P('grp', 'seq'), may hold values from -0.078125 to 0.078125
- up_weight: bfloat16 [5120, 13824], P('grp', 'seq'), may hold values from -0.078125 to 0.078125
- down_weight: bfloat16 [13824, 5120], P('seq', 'grp'), may hold values from -0.0546875 to 0.0546875
Outputs:
- mixed: bfloat16 [32, 4, 5120], P(None, None, ('grp', 'seq'))
The draws below stay inside these ranges and needn't reach their ends.
Inputs may be any that keep to these rules, and one draw needn't show every extreme that they name: `lengths`: one request holds exactly 16384 cached tokens. A permutation of the requests; request group_perm[i] belongs to group i // 4. `page_table`: page p of request r lies on the device with grp index g and seq index p // 8, where g is the group of r; the slots named for one device are all different.
All inputs are finite; a program needn't handle non-finite values.
Results may differ from the reference program's by a relative error of at most 0.015.
Values may be sent and summed in bfloat16 or wider, within the bound.
No kernel may reach another device: no remote copies, remote signals or barrier semaphores. Data moves between devices by JAX's collectives and lax.ppermute only.
A program may use at most 128 MiB of HBM per device.

```python
import math
import jax
import jax.numpy as jnp
from jax import lax

D = 5120
HEADS = 40
KV_HEADS = 8
HEAD_DIM = 128
FF = 13824
STEPS = 4
REQ_GRP = 4
SHARD_PAGES = 8
PAGE = 128
REQUESTS = 32
QKVW = 7168
POOL = 32
SLOTS = 4096
MAXPAGES = 128
MAXLEN = 16384
N_SEQ = 16
DEVICES = 128


def permute_slots(device_key):
    return jax.random.permutation(device_key, POOL)


def layout(key):
    order = jax.random.permutation(jax.random.fold_in(key, 101), REQUESTS).astype(jnp.int32)
    where_in = jnp.argsort(order).astype(jnp.int32)
    group_of = where_in // REQ_GRP
    member = where_in % REQ_GRP
    page_ids = jnp.arange(MAXPAGES, dtype=jnp.int32)
    shard_of = page_ids // SHARD_PAGES
    inside = page_ids % SHARD_PAGES
    device_of = group_of[:, None] * N_SEQ + shard_of[None, :]
    local_of = member[:, None] * SHARD_PAGES + inside[None, :]
    device_keys = jax.random.split(jax.random.fold_in(key, 102), DEVICES)
    shuffles = jax.vmap(permute_slots)(device_keys).astype(jnp.int32)
    return (order, shuffles[device_of, local_of].astype(jnp.int32))


def draw_group_perm(key, part):
    return layout(key)[0]


def draw_page_table(key, part):
    return layout(key)[1]


def draw_lengths(key, part):
    drawn = jax.random.randint(jax.random.fold_in(key, 103), (REQUESTS,), 1, MAXLEN + 1, dtype=jnp.int32)
    chosen = jax.random.randint(jax.random.fold_in(key, 104), (), 0, REQUESTS, dtype=jnp.int32)
    return drawn.at[chosen].set(MAXLEN)


def draw_tokens(key, part):
    shape = (REQUESTS, STEPS, D)
    columns = jnp.arange(D, dtype=jnp.float32) / D - 0.5
    row_scale = jnp.exp(jax.random.uniform(jax.random.fold_in(key, 301), (REQUESTS, STEPS, 1), jnp.float32, math.log(0.4), math.log(4.0)))
    jitter = jnp.exp(jax.random.uniform(jax.random.fold_in(key, 302), (D,), jnp.float32, math.log(0.6), math.log(1.7)))
    trend = 3.0 ** columns
    noise = jnp.clip(jax.random.normal(jax.random.fold_in(key, 305), shape, jnp.float32), -4.0, 4.0)
    return (noise * row_scale * trend * jitter).astype(jnp.bfloat16)


def draw_qkv_bias(key, part):
    values = jnp.clip(jax.random.normal(jax.random.fold_in(key, 202), (QKVW,), jnp.float32), -4.0, 4.0)
    return values


def draw_k_pool(key, part):
    shape = (SLOTS, PAGE, KV_HEADS * HEAD_DIM)
    values = 1.7 * jnp.clip(jax.random.normal(jax.random.fold_in(key, 207), shape, jnp.float32), -4.0, 4.0)
    return values.astype(jnp.bfloat16)


def levels(stream_key, extent, cuts, least, largest):
    factor_of = 1.0
    for axis_at, blocks in cuts:
        heights = jax.random.uniform(jax.random.fold_in(jax.random.fold_in(stream_key, 6), axis_at), (blocks,), jnp.float32, least / len(cuts), largest / len(cuts))
        factor_of = factor_of * jnp.repeat(jnp.exp(heights), extent[axis_at] // blocks).reshape((-1,) + (1,) * (len(extent) - 1 - axis_at))
    return factor_of


def bell_draw(own_key, shape, width, reach, pieces=(), kind=jnp.bfloat16):
    entries = width * jax.random.normal(own_key, shape, jnp.float32)
    if pieces:
        entries = entries * levels(own_key, shape, pieces, -0.22, 0.18)
    return jnp.clip(entries, -reach, reach).astype(kind)


def setup_inputs(seed: int = 0) -> dict:
    arg_keys = jax.random.split(jax.random.key(seed), 15)
    return {
        "tokens": draw_tokens(jax.random.fold_in(arg_keys[14], 71), 0),
        "lengths": draw_lengths(jax.random.fold_in(arg_keys[14], 71), 0),
        "group_perm": draw_group_perm(jax.random.fold_in(arg_keys[14], 71), 0),
        "page_table": draw_page_table(jax.random.fold_in(arg_keys[14], 71), 0),
        "k_pool": draw_k_pool(jax.random.fold_in(arg_keys[14], 71), 0),
        "v_pool": bell_draw(arg_keys[5], (SLOTS, PAGE, KV_HEADS * HEAD_DIM), 1.7, 7.0, ((0, 128),)),
        "gain_in": jnp.clip(1.0 + 0.15 * jax.random.normal(arg_keys[6], (D,), jnp.float32), 0.25, 1.75),
        "qkv_weight": bell_draw(arg_keys[7], (D, QKVW), (D // 3) ** -0.5, 0.15625, ((0, 8), (1, 16))),
        "qkv_bias": draw_qkv_bias(jax.random.fold_in(arg_keys[14], 71), 0),
        "o_weight": bell_draw(arg_keys[9], (HEADS * HEAD_DIM, D), (HEADS * HEAD_DIM) ** -0.5, 0.078125, ((0, 16), (1, 8))),
        "gain_mid": jnp.clip(1.0 + 0.15 * jax.random.normal(arg_keys[10], (D,), jnp.float32), 0.25, 1.75),
        "gate_weight": bell_draw(arg_keys[11], (D, FF), D ** -0.5, 0.078125, ((0, 8), (1, 16))),
        "up_weight": bell_draw(arg_keys[12], (D, FF), D ** -0.5, 0.078125, ((0, 8), (1, 16))),
        "down_weight": bell_draw(arg_keys[13], (FF, D), FF ** -0.5, 0.0546875, ((0, 16), (1, 8))),
    }


EPSILON = 1e-06
LOW_SCORE = -1e+30
ROPE_BASE = 1000000.0

def rotary(values, position):
    half_dim = values.shape[-1] // 2
    exponent = jnp.arange(half_dim, dtype=jnp.float32) * (2.0 / values.shape[-1])
    inverse = jnp.exp(-exponent * jnp.log(jnp.float32(ROPE_BASE)))
    angle = position[..., None, None] * inverse
    cosine = jnp.cos(angle)
    sine_part = jnp.sin(angle)
    first_half = values[..., :half_dim]
    second_half = values[..., half_dim:]
    return jnp.concatenate([first_half * cosine - second_half * sine_part, second_half * cosine + first_half * sine_part], axis=-1)

def rms_norm(values, gain):
    mean_square = lax.optimization_barrier(jnp.mean(values * values, axis=-1, keepdims=True))
    return (values * lax.rsqrt(mean_square + EPSILON) * gain).astype(jnp.bfloat16)

def reference(tokens, lengths, group_perm, page_table, k_pool, v_pool, gain_in, qkv_weight, qkv_bias, o_weight, gain_mid, gate_weight, up_weight, down_weight):
    q_width = HEADS * HEAD_DIM
    kv_width = KV_HEADS * HEAD_DIM
    group_q = HEADS // KV_HEADS
    query_rows = STEPS * group_q
    score_scale = HEAD_DIM ** (-0.5)
    inputs = tokens.astype(jnp.float32)
    normed_in = rms_norm(inputs, gain_in)
    projected = jnp.dot(normed_in.reshape(REQUESTS * STEPS, D), qkv_weight, preferred_element_type=jnp.float32)
    projected = projected.reshape(REQUESTS, STEPS, QKVW) + qkv_bias
    steps_range = jnp.arange(STEPS, dtype=jnp.int32)
    position = (lengths[:, None] + steps_range[None, :]).astype(jnp.float32)
    queries = rotary(projected[..., :q_width].reshape(REQUESTS, STEPS, HEADS, HEAD_DIM), position).astype(jnp.bfloat16)
    new_keys = rotary(projected[..., q_width:q_width + kv_width].reshape(REQUESTS, STEPS, KV_HEADS, HEAD_DIM), position).astype(jnp.bfloat16)
    new_values = projected[..., q_width + kv_width:].reshape(REQUESTS, STEPS, KV_HEADS, HEAD_DIM).astype(jnp.bfloat16)
    where_in = jnp.argsort(group_perm).astype(jnp.int32)
    group_of = where_in // REQ_GRP
    page_ids = jnp.arange(MAXPAGES, dtype=jnp.int32)
    slot_rows = (group_of[:, None] * N_SEQ + page_ids[None, :] // SHARD_PAGES) * POOL + page_table
    causal = (steps_range[None, :] <= (jnp.arange(query_rows, dtype=jnp.int32) // group_q)[:, None])[None]
    cache_positions = jnp.arange(MAXLEN, dtype=jnp.int32)

    def attend_one(item):
        slot_row, query_item, key_item, value_item, length = item
        cache_keys = k_pool[slot_row].reshape(MAXLEN, KV_HEADS, HEAD_DIM).astype(jnp.float32)
        cache_values = v_pool[slot_row].reshape(MAXLEN, KV_HEADS, HEAD_DIM).astype(jnp.float32)
        query_mat = query_item.reshape(STEPS, KV_HEADS, group_q, HEAD_DIM).transpose(1, 0, 2, 3).reshape(KV_HEADS, query_rows, HEAD_DIM).astype(jnp.float32)
        live_mask = (cache_positions < length)[None, None, :]
        cache_scores = jnp.einsum('hqd,khd->hqk', query_mat, cache_keys) * score_scale
        cache_scores = jnp.where(live_mask, cache_scores, LOW_SCORE)
        own_scores = jnp.einsum('hqd,khd->hqk', query_mat, key_item.astype(jnp.float32)) * score_scale
        own_scores = jnp.where(causal, own_scores, LOW_SCORE)
        top_score = jnp.maximum(lax.optimization_barrier(jnp.max(cache_scores, axis=-1)), lax.optimization_barrier(jnp.max(own_scores, axis=-1)))
        cache_weights = jnp.where(live_mask, jnp.exp(cache_scores - top_score[..., None]), 0.0)
        own_weights = jnp.where(causal, jnp.exp(own_scores - top_score[..., None]), 0.0)
        weight_sums = lax.optimization_barrier(jnp.sum(cache_weights, axis=-1)) + lax.optimization_barrier(jnp.sum(own_weights, axis=-1))
        cache_rounded = lax.optimization_barrier(cache_weights.astype(jnp.bfloat16)).astype(jnp.float32)
        own_rounded = lax.optimization_barrier(own_weights.astype(jnp.bfloat16)).astype(jnp.float32)
        weighted = jnp.einsum('hqk,khd->hqd', cache_rounded, cache_values) + jnp.einsum('hqk,khd->hqd', own_rounded, value_item.astype(jnp.float32))
        attended = weighted / weight_sums[..., None]
        return attended.reshape(KV_HEADS, STEPS, group_q, HEAD_DIM).transpose(1, 0, 2, 3).reshape(STEPS, q_width).astype(jnp.bfloat16)
    attended = lax.map(attend_one, (slot_rows, queries, new_keys, new_values, lengths))
    out_proj = jnp.dot(attended.reshape(REQUESTS * STEPS, q_width), o_weight, preferred_element_type=jnp.float32)
    residual = inputs + out_proj.reshape(REQUESTS, STEPS, D)
    normed_mid = rms_norm(residual, gain_mid).reshape(REQUESTS * STEPS, D)
    gate_sum = jnp.dot(normed_mid, gate_weight, preferred_element_type=jnp.float32)
    up_sum = jnp.dot(normed_mid, up_weight, preferred_element_type=jnp.float32)
    hidden = (jax.nn.silu(gate_sum) * up_sum).astype(jnp.bfloat16)
    down_sum = jnp.dot(hidden, down_weight, preferred_element_type=jnp.float32).reshape(REQUESTS, STEPS, D)
    return (residual + down_sum).astype(jnp.bfloat16)
```

```python
import functools

import jax
import jax.numpy as jnp
import numpy as np
from jax import lax
from jax.experimental import pallas as pl
from jax.experimental.pallas import tpu as pltpu
from jax.sharding import PartitionSpec as P

D = 5120
HEADS = 40
KV_HEADS = 8
HEAD_DIM = 128
STEPS = 4
REQ_GRP = 4
SHARD_PAGES = 8
PAGE = 128
REQUESTS = 32
ROWS = REQUESTS * STEPS
GROUP_ROWS = REQ_GRP * STEPS
N_GRP = 8
N_SEQ = 16
FEAT = D // (N_GRP * N_SEQ)
FEAT_PAD = 48
GFEAT = D // N_GRP
QCOLS = 448
QPAD = 512
OCOLS = 320
FCOLS = 864
FPAD = 896
QROWS = 24
SHARD_KEYS = SHARD_PAGES * PAGE
EPSILON = 1e-06
LOW_SCORE = -1e30
ROPE_BASE = 1000000.0
BF = jnp.bfloat16
F32 = jnp.float32


def call(kernel, outs, *args, smem=(), anys=(), scratch=()):
    specs = []
    for i in range(len(args)):
        if i in smem:
            specs.append(pl.BlockSpec(memory_space=pltpu.SMEM))
        elif i in anys:
            specs.append(pl.BlockSpec(memory_space=pl.ANY))
        else:
            specs.append(pl.BlockSpec(memory_space=pltpu.VMEM))
    many = isinstance(outs, (list, tuple))
    vm = pl.BlockSpec(memory_space=pltpu.VMEM)
    return pl.pallas_call(
        kernel,
        out_shape=outs,
        in_specs=specs,
        out_specs=[vm] * len(outs) if many else vm,
        scratch_shapes=list(scratch),
        name=getattr(kernel, "__name__", "kernel"),
        compiler_params=pltpu.CompilerParams(vmem_limit_bytes=48 << 20),
    )(*args)


def sds(shape, dtype=BF):
    return jax.ShapeDtypeStruct(shape, dtype)


def split(value):
    hi = value.astype(BF).astype(F32)
    return hi, value - hi


def iota(shape, axis):
    return lax.broadcasted_iota(jnp.int32, shape, axis)


def spread_features(value, squares, out_ref):
    hi, lo = split(squares)
    tail = jnp.where(iota((8, ROWS), 0) == 0, hi, jnp.where(iota((8, ROWS), 0) == 1, lo, 0.0))
    block = jnp.concatenate([value, tail], axis=0).astype(BF)
    for s in range(N_SEQ):
        out_ref[s] = block


def start_kernel(perm_ref, tok_ref, gain_ref, send_ref, xt_ref, hot_ref):
    lane = iota((8, ROWS), 1)
    source = lane & (STEPS - 1)
    for n in range(REQUESTS):
        source = source + jnp.where((lane >> 2) == n, perm_ref[n] * STEPS, 0)
    hot = jnp.where(iota((ROWS, ROWS), 0) == source[0:1, :], 1.0, 0.0).astype(BF)
    hot_ref[...] = hot
    xt = lax.dot_general(tok_ref[...], hot, (((0,), (0,)), ((), ())), preferred_element_type=F32)
    xt_ref[...] = xt
    squares = jnp.sum(xt * xt, axis=0, keepdims=True)
    spread_features(xt * gain_ref[...], squares, send_ref)


def collect_features(in_ref, scratch):
    squares = jnp.zeros((1, ROWS), F32)
    for s in range(N_SEQ):
        block = in_ref[s].astype(F32)
        scratch[s * FEAT : (s + 1) * FEAT, :] = block[:FEAT]
        squares = squares + block[FEAT : FEAT + 1] + block[FEAT + 1 : FEAT + 2]
    value = scratch[...].T.astype(BF)
    squares = jnp.broadcast_to(squares, (ROWS, ROWS)).T
    return value, squares


def qkv_kernel(in_ref, w_ref, out_ref, scratch):
    value, squares = collect_features(in_ref, scratch)
    part = jnp.dot(value, w_ref[...], preferred_element_type=F32)
    hi, lo = split(squares)
    for g in range(N_GRP):
        rows = slice(g * GROUP_ROWS, (g + 1) * GROUP_ROWS)
        out_ref[g, :, :QCOLS] = part[rows].astype(BF)
        out_ref[g, :, QCOLS:] = jnp.where(
            iota((GROUP_ROWS, QPAD - QCOLS), 1) < 32, hi[rows, : QPAD - QCOLS], lo[rows, : QPAD - QCOLS]
        ).astype(BF)


def scale_of(total, at):
    squares = total[:, at : at + 1] + total[:, at + 16 : at + 17]
    return lax.rsqrt(squares / D + EPSILON)


def qkv_sum_kernel(in_ref, bias_ref, out_ref):
    total = in_ref[0].astype(F32)
    for g in range(1, N_GRP):
        total = total + in_ref[g].astype(F32)
    squares = total[:, QCOLS : QCOLS + 1] + total[:, QCOLS + 32 : QCOLS + 33]
    scale = lax.rsqrt(squares / D + EPSILON)
    value = total * scale + bias_ref[...]
    value = jnp.where(iota(value.shape, 1) < QCOLS, value, 0.0)
    odd = lax.rem(lax.axis_index("seq"), 2) == 1
    value = jnp.where(odd, pltpu.roll(value, QPAD - QCOLS, 1), value).astype(BF)
    for s in range(N_SEQ):
        out_ref[s] = value


def attend_kernel(
    perm_ref, len_ref, page_ref, in_ref, cos_ref, sin_ref, k_hbm, v_hbm, out_ref,
    kbuf, vbuf, qbuf, knew, vnew, rot, sems,
):
    grp_idx = lax.axis_index("grp")
    seq_idx = lax.axis_index("seq")

    def copies(r, p):
        slot = page_ref[perm_ref[grp_idx * REQ_GRP + r], seq_idx * SHARD_PAGES + p]
        rows = pl.ds(p * PAGE, PAGE)
        return (
            pltpu.make_async_copy(k_hbm.at[slot], kbuf.at[r, rows], sems.at[r, p, 0]),
            pltpu.make_async_copy(v_hbm.at[slot], vbuf.at[r, rows], sems.at[r, p, 1]),
        )

    for r in range(REQ_GRP):
        for p in range(SHARD_PAGES):
            for copy in copies(r, p):
                copy.start()

    for r in range(REQ_GRP):
        member = perm_ref[grp_idx * REQ_GRP + r]
        rot[0, r * STEPS : (r + 1) * STEPS, :] = cos_ref[member]
        rot[1, r * STEPS : (r + 1) * STEPS, :] = sin_ref[member]
    cosine = rot[0]
    sine = rot[1]
    knew[...] = jnp.zeros_like(knew)
    vnew[...] = jnp.zeros_like(vnew)
    qbuf[...] = jnp.zeros_like(qbuf)
    for pair in range(N_SEQ // 2):
        even = in_ref[2 * pair].astype(F32)
        odd = in_ref[2 * pair + 1].astype(F32)
        for k in range(7):
            lanes = slice(k * 128, (k + 1) * 128)
            olanes = slice((k - 3) * 128, (k - 2) * 128)
            if k < 3:
                value = even[:, lanes]
            elif k == 3:
                value = even[:, lanes] + odd[:, olanes]
            else:
                value = odd[:, olanes]
            head = pair * 7 + k
            if head < HEADS + KV_HEADS:
                value = value * cosine + pltpu.roll(value, HEAD_DIM // 2, 1) * sine
            if head < HEADS:
                h, j = divmod(head, HEADS // KV_HEADS)
                for r in range(REQ_GRP):
                    qbuf[r, h * QROWS + j * STEPS : h * QROWS + (j + 1) * STEPS, :] = value[
                        r * STEPS : (r + 1) * STEPS
                    ]
            elif head < HEADS + KV_HEADS:
                h = head - HEADS
                knew[:GROUP_ROWS, h * HEAD_DIM : (h + 1) * HEAD_DIM] = value.astype(BF)
            else:
                h = head - HEADS - KV_HEADS
                vnew[:GROUP_ROWS, h * HEAD_DIM : (h + 1) * HEAD_DIM] = value.astype(BF)

    score_scale = HEAD_DIM ** (-0.5)
    step = iota((QROWS, PAGE), 0) & (STEPS - 1)
    column = iota((QROWS, PAGE), 1)
    place = iota((QROWS, SHARD_KEYS), 1)
    lane = iota((QROWS, HEAD_DIM), 1)
    is_last = seq_idx == N_SEQ - 1
    nt = (((1,), (1,)), ((), ()))

    def one(r, carry):
        for p in range(SHARD_PAGES):
            for copy in copies(r, p):
                copy.wait()
        live = len_ref[perm_ref[grp_idx * REQ_GRP + r]] - seq_idx * SHARD_KEYS
        live_mask = place < live
        own_mask = ((column >> 2) == r) & ((column & (STEPS - 1)) <= step) & is_last & (column < GROUP_ROWS)
        for h in range(KV_HEADS):
            lanes = slice(h * HEAD_DIM, (h + 1) * HEAD_DIM)
            query = qbuf[r, h * QROWS : (h + 1) * QROWS, :].astype(BF)
            scores = lax.dot_general(query, kbuf[r, :, lanes], nt, preferred_element_type=F32)
            scores = jnp.where(live_mask, scores * score_scale, LOW_SCORE)
            own = lax.dot_general(query, knew[:, lanes], nt, preferred_element_type=F32)
            own = jnp.where(own_mask, own * score_scale, LOW_SCORE)
            best = jnp.maximum(
                jnp.max(scores, axis=1, keepdims=True), jnp.max(own, axis=1, keepdims=True)
            )
            weight = jnp.where(live_mask, jnp.exp(scores - best), 0.0)
            own_weight = jnp.where(own_mask, jnp.exp(own - best), 0.0)
            total = jnp.sum(weight, axis=1, keepdims=True) + jnp.sum(own_weight, axis=1, keepdims=True)
            mixed = jnp.dot(
                weight.astype(BF), vbuf[r, :, lanes], preferred_element_type=F32
            ) + jnp.dot(own_weight.astype(BF), vnew[:, lanes], preferred_element_type=F32)
            some = total > 0.0
            safe = jnp.where(some, total, 1.0)
            mixed = mixed / safe
            level = jnp.where(some, best + jnp.log(safe), LOW_SCORE)
            hi, rest = split(level)
            mid, low = split(rest)
            level = jnp.where(lane < 32, hi, jnp.where(lane < 64, mid, low))
            both = jnp.concatenate([mixed[:16], level[:16]], axis=0)
            out_ref[2 * h, r] = both.astype(BF)
            both = jnp.concatenate([mixed[8:], level[8:]], axis=0)
            out_ref[2 * h + 1, r] = both.astype(BF)
        return carry

    lax.fori_loop(0, REQ_GRP, one, 0)


def merge_kernel(in_ref, out_ref, scratch):
    for r in range(REQ_GRP):
        levels = []
        for s in range(N_SEQ):
            cols = in_ref[s, r, 16:, :].astype(F32)
            levels.append(cols[:, 0:1] + cols[:, 32:33] + cols[:, 64:65])
        best = functools.reduce(jnp.maximum, levels)
        total = jnp.zeros_like(best)
        value = jnp.zeros((16, HEAD_DIM), F32)
        for s in range(N_SEQ):
            factor = jnp.exp(levels[s] - best)
            total = total + factor
            value = value + in_ref[s, r, :16, :].astype(F32) * factor
        value = value / total
        for j in range(3):
            scratch[r * STEPS : (r + 1) * STEPS, j * HEAD_DIM : (j + 1) * HEAD_DIM] = value[
                j * STEPS : (j + 1) * STEPS
            ]
    value = scratch[...]
    odd = lax.rem(lax.axis_index("seq"), 2) == 1
    value = jnp.where(odd, pltpu.roll(value, 3 * HEAD_DIM - HEAD_DIM // 2, 1), value).astype(BF)
    for g in range(N_GRP):
        out_ref[g] = value


def send_back(part, out_ref):
    turned = part.T
    for s in range(N_SEQ):
        out_ref[s] = turned[s * FEAT : (s + 1) * FEAT].astype(BF)


def project_kernel(in_ref, w_ref, out_ref):
    value = in_ref[...].reshape(ROWS, in_ref.shape[2])[:, : w_ref.shape[0]]
    send_back(jnp.dot(value, w_ref[...], preferred_element_type=F32), out_ref)


def middle_kernel(in_ref, xt_ref, gain_ref, send_ref, res_ref):
    total = xt_ref[...]
    part = in_ref[0].astype(F32)
    for s in range(1, N_SEQ):
        part = part + in_ref[s].astype(F32)
    total = total + part
    res_ref[...] = total
    squares = jnp.sum(total * total, axis=0, keepdims=True)
    spread_features(total * gain_ref[...], squares, send_ref)


def gate_kernel(in_ref, gate_ref, up_ref, out_ref, scratch):
    value, squares = collect_features(in_ref, scratch)
    gate = jnp.dot(value, gate_ref[...], preferred_element_type=F32)
    up = jnp.dot(value, up_ref[...], preferred_element_type=F32)
    hi, lo = split(squares)
    for g in range(N_GRP):
        rows = slice(g * GROUP_ROWS, (g + 1) * GROUP_ROWS)
        out_ref[g, :, :FCOLS] = gate[rows].astype(BF)
        out_ref[g, :, FCOLS:FPAD] = jnp.where(
            iota((GROUP_ROWS, FPAD - FCOLS), 1) < 16, hi[rows, : FPAD - FCOLS], lo[rows, : FPAD - FCOLS]
        ).astype(BF)
        out_ref[g, :, FPAD : FPAD + FCOLS] = up[rows].astype(BF)
        out_ref[g, :, FPAD + FCOLS :] = jnp.zeros((GROUP_ROWS, FPAD - FCOLS), BF)


def hidden_kernel(in_ref, out_ref):
    total = in_ref[0].astype(F32)
    for g in range(1, N_GRP):
        total = total + in_ref[g].astype(F32)
    scale = scale_of(total, FCOLS)
    gate = total[:, :FPAD] * scale
    up = total[:, FPAD:] * scale
    value = (gate / (1.0 + jnp.exp(-gate)) * up).astype(BF)
    for g in range(N_GRP):
        out_ref[g] = value


def finish_kernel(in_ref, res_ref, hot_ref, out_ref):
    part = in_ref[0].astype(F32)
    for s in range(1, N_SEQ):
        part = part + in_ref[s].astype(F32)
    total = (res_ref[...] + part).astype(BF)
    out_ref[...] = lax.dot_general(
        hot_ref[...], total, (((1,), (1,)), ((), ())), preferred_element_type=F32
    ).astype(BF)


def exchange(value, axis):
    return lax.all_to_all(value, axis, 0, 0, tiled=False)


def body(
    tokens, lengths, group_perm, page_table, k_pool, v_pool, gain_in, qkv_weight, qkv_bias,
    o_weight, gain_mid, gate_weight, up_weight, down_weight,
):
    half = HEAD_DIM // 2
    inverse = np.exp(-np.arange(half) * (2.0 / HEAD_DIM) * np.log(ROPE_BASE)).astype(np.float32)
    inverse = jnp.asarray(np.concatenate([inverse, inverse]))
    position = (lengths[:, None] + jnp.arange(STEPS, dtype=jnp.int32)[None, :]).astype(F32)
    angle = position[..., None] * inverse
    cosine = jnp.cos(angle)
    sine = jnp.where(jnp.arange(HEAD_DIM) < half, -1.0, 1.0) * jnp.sin(angle)

    send, xt, hot = call(
        start_kernel,
        [sds((N_SEQ, FEAT_PAD, ROWS)), sds((FEAT, ROWS), F32), sds((ROWS, ROWS))],
        group_perm, tokens.reshape(ROWS, FEAT), gain_in[:, None],
        smem=(0,),
    )
    got = exchange(send, "seq")
    send = call(
        qkv_kernel, sds((N_GRP, GROUP_ROWS, QPAD)), got, qkv_weight,
        scratch=[pltpu.VMEM((GFEAT, ROWS), F32)],
    )
    got = exchange(send, "grp")
    bias = jnp.pad(qkv_bias, (0, QPAD - QCOLS))[None, :]
    send = call(qkv_sum_kernel, sds((N_SEQ, GROUP_ROWS, QPAD)), got, bias)
    got = exchange(send, "seq")
    send = call(
        attend_kernel, sds((N_SEQ, REQ_GRP, 32, HEAD_DIM)),
        group_perm, lengths, page_table, got, cosine, sine, k_pool, v_pool,
        smem=(0, 1, 2), anys=(6, 7),
        scratch=[
            pltpu.VMEM((REQ_GRP, SHARD_KEYS, KV_HEADS * HEAD_DIM), BF),
            pltpu.VMEM((REQ_GRP, SHARD_KEYS, KV_HEADS * HEAD_DIM), BF),
            pltpu.VMEM((REQ_GRP, KV_HEADS * QROWS, HEAD_DIM), F32),
            pltpu.VMEM((PAGE, KV_HEADS * HEAD_DIM), BF),
            pltpu.VMEM((PAGE, KV_HEADS * HEAD_DIM), BF),
            pltpu.VMEM((2, GROUP_ROWS, HEAD_DIM), F32),
            pltpu.SemaphoreType.DMA((REQ_GRP, SHARD_PAGES, 2)),
        ],
    )
    got = exchange(send, "seq")
    send = call(
        merge_kernel, sds((N_GRP, GROUP_ROWS, 3 * HEAD_DIM)), got,
        scratch=[pltpu.VMEM((GROUP_ROWS, 3 * HEAD_DIM), F32)],
    )
    got = exchange(send, "grp")
    send = call(project_kernel, sds((N_SEQ, FEAT, ROWS)), got, o_weight)
    got = exchange(send, "seq")
    send, res = call(
        middle_kernel, [sds((N_SEQ, FEAT_PAD, ROWS)), sds((FEAT, ROWS), F32)],
        got, xt, gain_mid[:, None],
    )
    got = exchange(send, "seq")
    send = call(
        gate_kernel, sds((N_GRP, GROUP_ROWS, 2 * FPAD)), got, gate_weight, up_weight,
        scratch=[pltpu.VMEM((GFEAT, ROWS), F32)],
    )
    got = exchange(send, "grp")
    send = call(hidden_kernel, sds((N_GRP, GROUP_ROWS, FPAD)), got)
    got = exchange(send, "grp")
    send = call(project_kernel, sds((N_SEQ, FEAT, ROWS)), got, down_weight)
    got = exchange(send, "seq")
    out = call(finish_kernel, sds((ROWS, FEAT)), got, res, hot)
    return out.reshape(REQUESTS, STEPS, FEAT)


def solution(mesh):
    return jax.shard_map(
        body,
        mesh=mesh,
        in_specs=(
            P(None, None, ("grp", "seq")),
            P(),
            P(),
            P(),
            P(("grp", "seq"), None, None),
            P(("grp", "seq"), None, None),
            P(("grp", "seq")),
            P("grp", "seq"),
            P("seq"),
            P("seq", "grp"),
            P(("grp", "seq")),
            P("grp", "seq"),
            P("grp", "seq"),
            P("seq", "grp"),
        ),
        out_specs=P(None, None, ("grp", "seq")),
        check_vma=False,
    )
```

```python
import functools

import jax
import jax.numpy as jnp
import numpy as np
from jax import lax
from jax.experimental import pallas as pl
from jax.experimental.pallas import tpu as pltpu
from jax.sharding import PartitionSpec as P

D = 5120
HEADS = 40
KV_HEADS = 8
HEAD_DIM = 128
STEPS = 4
AHEAD = 2
REQ_GRP = 4
SHARD_PAGES = 8
PAGE = 128
REQUESTS = 32
ROWS = REQUESTS * STEPS
GROUP_ROWS = REQ_GRP * STEPS
N_GRP = 8
N_SEQ = 16
N_CHIP = N_GRP // 2
FEAT = D // (N_GRP * N_SEQ)
FEAT_PAD = 48
GFEAT = D // N_GRP
QCOLS = 448
QPAD = 512
OCOLS = 320
FCOLS = 864
FPAD = 896
QROWS = 24
SHARD_KEYS = SHARD_PAGES * PAGE
EPSILON = 1e-06
LOW_SCORE = -1e30
ROPE_BASE = 1000000.0
BF = jnp.bfloat16
F32 = jnp.float32


def call(kernel, outs, *args, smem=(), anys=(), scratch=()):
    specs = []
    for i in range(len(args)):
        if i in smem:
            specs.append(pl.BlockSpec(memory_space=pltpu.SMEM))
        elif i in anys:
            specs.append(pl.BlockSpec(memory_space=pltpu.HBM))
        else:
            specs.append(pl.BlockSpec(memory_space=pltpu.VMEM))
    args = [pltpu.with_memory_space_constraint(v, pltpu.HBM) if i in anys else v for i, v in enumerate(args)]
    many = isinstance(outs, (list, tuple))
    vm = pl.BlockSpec(memory_space=pltpu.VMEM)
    return pl.pallas_call(
        kernel,
        out_shape=outs,
        in_specs=specs,
        out_specs=[vm] * len(outs) if many else vm,
        scratch_shapes=list(scratch),
        name=getattr(kernel, "__name__", "kernel"),
        compiler_params=pltpu.CompilerParams(vmem_limit_bytes=32 << 20),
    )(*args)


def sds(shape, dtype=BF):
    return jax.ShapeDtypeStruct(shape, dtype)


def split(value):
    hi = value.astype(BF).astype(F32)
    return hi, value - hi


def iota(shape, axis):
    return lax.broadcasted_iota(jnp.int32, shape, axis)


def spread_features(value, squares, out_ref):
    hi, lo = split(squares)
    tail = jnp.where(iota((8, ROWS), 0) == 0, hi, jnp.where(iota((8, ROWS), 0) == 1, lo, 0.0))
    block = jnp.concatenate([value, tail], axis=0).astype(BF)
    for s in range(N_SEQ):
        out_ref[s] = block


def start_kernel(perm_hbm, tok_hbm, gain_hbm, send_ref, xt_ref, hot_ref, perm_ref, tok_ref, gain_ref, sems):
    copies = [
        pltpu.make_async_copy(perm_hbm, perm_ref, sems.at[0]),
        pltpu.make_async_copy(tok_hbm, tok_ref, sems.at[1]),
        pltpu.make_async_copy(gain_hbm, gain_ref, sems.at[2]),
    ]
    for copy in copies:
        copy.start()
    for copy in copies:
        copy.wait()
    lane = iota((8, ROWS), 1)
    source = lane & (STEPS - 1)
    for n in range(REQUESTS):
        source = source + jnp.where((lane >> 2) == n, perm_ref[n] * STEPS, 0)
    hot = jnp.where(iota((ROWS, ROWS), 0) == source[0:1, :], 1.0, 0.0).astype(BF)
    hot_ref[...] = hot
    tok = tok_ref[...]
    scaled = (tok.astype(F32) * gain_ref[...]).astype(BF)
    turn = (((0,), (0,)), ((), ()))
    xt = lax.dot_general(tok, hot, turn, preferred_element_type=F32)
    xt_ref[...] = xt
    squares = jnp.sum(xt * xt, axis=0, keepdims=True)
    spread_features(lax.dot_general(scaled, hot, turn, preferred_element_type=F32), squares, send_ref)


def collect_features(in_ref, scratch):
    squares = jnp.zeros((1, ROWS), F32)
    for s in range(N_SEQ):
        block = in_ref[s].astype(F32)
        scratch[s * FEAT : (s + 1) * FEAT, :] = block[:FEAT]
        squares = squares + block[FEAT : FEAT + 1] + block[FEAT + 1 : FEAT + 2]
    value = scratch[...].T.astype(BF)
    squares = jnp.broadcast_to(squares, (ROWS, ROWS)).T
    return value, squares


def qkv_kernel(in_ref, w_ref, out_ref, scratch):
    value, squares = collect_features(in_ref, scratch)
    part = jnp.dot(value, w_ref[...], preferred_element_type=F32)
    hi, lo = split(squares)
    for g in range(N_GRP):
        rows = slice(g * GROUP_ROWS, (g + 1) * GROUP_ROWS)
        out_ref[g, :, :QCOLS] = part[rows].astype(BF)
        out_ref[g, :, QCOLS:] = jnp.where(
            iota((GROUP_ROWS, QPAD - QCOLS), 1) < 32, hi[rows, : QPAD - QCOLS], lo[rows, : QPAD - QCOLS]
        ).astype(BF)


def scale_of(total, at):
    squares = total[:, at : at + 1] + total[:, at + 16 : at + 17]
    return lax.rsqrt(squares / D + EPSILON)


def qkv_sum_kernel(in_ref, bias_ref, out_ref):
    total = in_ref[0].astype(F32)
    for g in range(1, N_GRP):
        total = total + in_ref[g].astype(F32)
    squares = total[:, QCOLS : QCOLS + 1] + total[:, QCOLS + 32 : QCOLS + 33]
    scale = lax.rsqrt(squares / D + EPSILON)
    value = total * scale + bias_ref[...]
    value = jnp.where(iota(value.shape, 1) < QCOLS, value, 0.0)
    odd = lax.rem(lax.axis_index("seq"), 2) == 1
    value = jnp.where(odd, pltpu.roll(value, QPAD - QCOLS, 1), value).astype(BF)
    for s in range(N_SEQ):
        out_ref[s] = value


def attend_kernel(
    perm_ref, len_ref, page_ref, in_ref, cos_ref, sin_ref, k_hbm, v_hbm, out_ref,
    qbuf, knew, vnew, rot, sbuf, obuf, kbuf, vbuf, sems,
):
    grp_idx = lax.axis_index("grp")
    seq_idx = lax.axis_index("seq")
    members = [perm_ref[grp_idx * REQ_GRP + r] for r in range(REQ_GRP)]
    copies = [[], []]
    for r in range(REQ_GRP):
        for kind, (pool, buf) in enumerate(((k_hbm, kbuf), (v_hbm, vbuf))):
            pages = []
            for p in range(SHARD_PAGES):
                slot = page_ref[members[r], seq_idx * SHARD_PAGES + p]
                to = buf.at[r, pl.ds(p * PAGE, PAGE)]
                pages.append(pltpu.make_async_copy(pool.at[slot], to, sems.at[kind, r]))
            copies[kind].append(pages)

    def begin(kind, r):
        if r < REQ_GRP:
            for copy in copies[kind][r]:
                copy.start()

    def await_pages(kind, r):
        whole = (kbuf, vbuf)[kind].at[r]
        pltpu.make_async_copy(whole, whole, sems.at[kind, r]).wait()

    for r in range(AHEAD):
        begin(0, r)
        begin(1, r)
    for r in range(REQ_GRP):
        rot[0, r * STEPS : (r + 1) * STEPS, :] = cos_ref[members[r]]
        rot[1, r * STEPS : (r + 1) * STEPS, :] = sin_ref[members[r]]
    cosine = rot[0]
    sine = rot[1]
    knew[...] = jnp.zeros_like(knew)
    vnew[...] = jnp.zeros_like(vnew)
    qbuf[...] = jnp.zeros_like(qbuf)
    for pair in range(N_SEQ // 2):
        even = in_ref[2 * pair].astype(F32)
        odd = in_ref[2 * pair + 1].astype(F32)
        for k in range(7):
            lanes = slice(k * 128, (k + 1) * 128)
            olanes = slice((k - 3) * 128, (k - 2) * 128)
            if k < 3:
                value = even[:, lanes]
            elif k == 3:
                value = even[:, lanes] + odd[:, olanes]
            else:
                value = odd[:, olanes]
            head = pair * 7 + k
            if head < HEADS + KV_HEADS:
                value = value * cosine + pltpu.roll(value, HEAD_DIM // 2, 1) * sine
            if head < HEADS:
                h, j = divmod(head, HEADS // KV_HEADS)
                for r in range(REQ_GRP):
                    at = h * QROWS + j * STEPS
                    side = (h % 2) * HEAD_DIM
                    qbuf[r, at : at + STEPS, side : side + HEAD_DIM] = value[r * STEPS : (r + 1) * STEPS]
            elif head < HEADS + KV_HEADS:
                h = head - HEADS
                knew[:GROUP_ROWS, h * HEAD_DIM : (h + 1) * HEAD_DIM] = value.astype(BF)
            else:
                h = head - HEADS - KV_HEADS
                vnew[:GROUP_ROWS, h * HEAD_DIM : (h + 1) * HEAD_DIM] = value.astype(BF)

    score_scale = HEAD_DIM ** (-0.5)
    power = score_scale * float(np.log2(np.e))
    step = iota((2 * QROWS, PAGE), 0) & (STEPS - 1)
    column = iota((2 * QROWS, PAGE), 1)
    own_live = ((column & (STEPS - 1)) <= step) & (seq_idx == N_SEQ - 1) & (column < GROUP_ROWS)
    place = iota((8, SHARD_KEYS), 1)
    group = iota((2 * QROWS, HEAD_DIM), 1) >> 3
    word = lax.rem(group, 3)
    part_lane = iota((STEPS, HEAD_DIM), 1)
    nt = (((1,), (1,)), ((), ()))
    for r in range(REQ_GRP):
        await_pages(0, r)
        begin(0, r + AHEAD)
        live = len_ref[members[r]] - seq_idx * SHARD_KEYS
        bias = jnp.where(place < live, 0.0, LOW_SCORE)[0:1]
        own_bias = jnp.where(own_live & ((column >> 2) == r), 0.0, LOW_SCORE)
        for h in range(0, KV_HEADS, 2):
            lanes = slice(h * HEAD_DIM, (h + 2) * HEAD_DIM)
            rows = slice(h * QROWS, (h + 2) * QROWS)
            query = qbuf[r, rows, :].astype(BF)
            scores = lax.dot_general(query, kbuf[r, :, lanes], nt, preferred_element_type=F32)
            sbuf[rows, :SHARD_KEYS] = scores + bias
            own = lax.dot_general(query, knew[:, lanes], nt, preferred_element_type=F32)
            sbuf[rows, SHARD_KEYS:] = own + own_bias
        await_pages(1, r)
        begin(1, r + AHEAD)
        for pair in range(0, KV_HEADS, 2):
            lanes = slice(pair * HEAD_DIM, (pair + 2) * HEAD_DIM)
            scores = sbuf[pair * QROWS : (pair + 2) * QROWS, :]
            best = jnp.max(scores, axis=1, keepdims=True)
            weight = jnp.exp2((scores - best) * power)
            total = jnp.sum(weight, axis=1, keepdims=True)
            weight = weight.astype(BF)
            both = jnp.dot(
                weight[:, :SHARD_KEYS], vbuf[r, :, lanes], preferred_element_type=F32
            ) + jnp.dot(weight[:, SHARD_KEYS:], vnew[:, lanes], preferred_element_type=F32)
            both = both / total
            levels = jnp.where(best > 0.1 * LOW_SCORE, best * score_scale + jnp.log(total), LOW_SCORE)
            hi, rest = split(levels)
            mid, low = split(rest)
            levels = jnp.where(word == 0, hi, jnp.where(word == 1, mid, low))
            for side in range(2):
                h = pair + side
                mixed = both[side * QROWS : (side + 1) * QROWS, side * HEAD_DIM : (side + 1) * HEAD_DIM]
                level = levels[side * QROWS : (side + 1) * QROWS]
                for half in range(2):
                    to = slice(r * STEPS, (r + 1) * STEPS)
                    parts = [slice((2 * half + j) * STEPS, (2 * half + j + 1) * STEPS) for j in range(3)]
                    for j in range(3):
                        obuf[2 * h + half, to, j * HEAD_DIM : (j + 1) * HEAD_DIM] = mixed[parts[j]]
                    obuf[2 * h + half, to, 3 * HEAD_DIM :] = jnp.where(
                        part_lane < 24, level[parts[0]], jnp.where(part_lane < 48, level[parts[1]], level[parts[2]])
                    )
    for s in range(N_SEQ):
        out_ref[s] = obuf[s].astype(BF)


def merge_kernel(in_ref, out_ref):
    levels = []
    for s in range(N_SEQ):
        cols = in_ref[s, :, 3 * HEAD_DIM :].astype(F32)
        levels.append(
            [cols[:, a : a + 1] + cols[:, a + 8 : a + 9] + cols[:, a + 16 : a + 17] for a in (0, 24, 48)]
        )
    out = []
    for j in range(3):
        best = functools.reduce(jnp.maximum, [level[j] for level in levels])
        total = jnp.zeros_like(best)
        value = jnp.zeros((GROUP_ROWS, HEAD_DIM), F32)
        for s in range(N_SEQ):
            factor = jnp.exp(levels[s][j] - best)
            total = total + factor
            value = value + in_ref[s, :, j * HEAD_DIM : (j + 1) * HEAD_DIM].astype(F32) * factor
        out.append(value / total)
    value = jnp.concatenate(out, axis=1)
    odd = lax.rem(lax.axis_index("seq"), 2) == 1
    value = jnp.where(odd, pltpu.roll(value, 3 * HEAD_DIM - HEAD_DIM // 2, 1), value).astype(BF)
    for g in range(N_GRP):
        out_ref[g] = value


def send_back(part, out_ref):
    turned = part.T
    for s in range(N_SEQ):
        out_ref[s] = turned[s * FEAT : (s + 1) * FEAT].astype(BF)


def on_second_core():
    return lax.rem(lax.axis_index("grp"), 2) == 1


def on_second_core():
    return lax.rem(lax.axis_index("grp"), 2) == 1


def project_kernel(in_ref, w_ref, out_ref):
    value = in_ref[...].reshape(ROWS, in_ref.shape[2])[:, : w_ref.shape[0]]
    send_back(jnp.dot(value, w_ref[...], preferred_element_type=F32), out_ref)


def middle_kernel(in_ref, xt_ref, gain_ref, send_ref, res_ref):
    total = xt_ref[...]
    part = in_ref[0].astype(F32)
    for s in range(1, N_SEQ):
        part = part + in_ref[s].astype(F32)
    total = total + part
    res_ref[...] = total
    squares = jnp.sum(total * total, axis=0, keepdims=True)
    spread_features(total * gain_ref[...], squares, send_ref)


def gate_kernel(in_ref, gate_ref, up_ref, keep_ref, give_ref, scratch):
    value, squares = collect_features(in_ref, scratch)
    gate = jnp.dot(value, gate_ref[...], preferred_element_type=F32)
    up = jnp.dot(value, up_ref[...], preferred_element_type=F32)
    hi, lo = split(squares)
    tail = FPAD - FCOLS
    sums = jnp.where(iota((ROWS, tail), 1) < tail // 2, hi[:, :tail], lo[:, :tail])
    second = on_second_core()
    spare = slice(FCOLS, FPAD)
    for x in range(N_CHIP):
        first_rows = slice(2 * x * GROUP_ROWS, (2 * x + 1) * GROUP_ROWS)
        last_rows = slice((2 * x + 1) * GROUP_ROWS, (2 * x + 2) * GROUP_ROWS)
        for lanes, part in (
            (slice(0, FCOLS), gate),
            (spare, sums),
            (slice(FPAD, FPAD + FCOLS), up),
        ):
            first = part[first_rows]
            last = part[last_rows]
            keep_ref[x, :, lanes] = jnp.where(second, last, first)
            give_ref[x, :, lanes] = jnp.where(second, first, last).astype(BF)
        keep_ref[x, :, FPAD + FCOLS :] = jnp.zeros((GROUP_ROWS, tail), F32)
        give_ref[x, :, FPAD + FCOLS :] = jnp.zeros((GROUP_ROWS, tail), BF)


def pair_kernel(keep_ref, got_ref, out_ref):
    tail = (FPAD - FCOLS) // 2
    start = FPAD - 128
    lane = iota((GROUP_ROWS, 128), 1)
    for x in range(N_CHIP):
        total = keep_ref[x] + got_ref[x].astype(F32)
        out_ref[x] = total.astype(BF)
        last = total[:, start:FPAD]
        hi, lo = split(last + pltpu.roll(last, 128 - tail, 1))
        last = jnp.where(
            lane < 128 - 2 * tail, last, jnp.where(lane < 128 - tail, hi, pltpu.roll(lo, tail, 1))
        )
        out_ref[x, :, start:FPAD] = last.astype(BF)


def hidden_kernel(in_ref, out_ref):
    total = in_ref[0].astype(F32)
    for x in range(1, N_CHIP):
        total = total + in_ref[x].astype(F32)
    scale = scale_of(total, FCOLS)
    gate = total[:, :FPAD] * scale
    up = total[:, FPAD:] * scale
    value = (gate / (1.0 + jnp.exp(-gate)) * up).astype(BF)
    for g in range(N_GRP):
        out_ref[g] = value


def finish_kernel(in_ref, res_ref, hot_ref, out_ref):
    part = in_ref[0].astype(F32)
    for s in range(1, N_SEQ):
        part = part + in_ref[s].astype(F32)
    total = (res_ref[...] + part).astype(BF)
    out_ref[...] = lax.dot_general(
        hot_ref[...], total, (((1,), (1,)), ((), ())), preferred_element_type=F32
    ).astype(BF)


def exchange(value, axis):
    return lax.all_to_all(value, axis, 0, 0, tiled=False)


def exchange_chips(value):
    groups = [list(range(core, N_GRP, 2)) for core in range(2)]
    return lax.all_to_all(value, "grp", 0, 0, axis_index_groups=groups, tiled=False)


def swap_cores(value):
    return lax.ppermute(value, "grp", [(i, i ^ 1) for i in range(N_GRP)])


def body(
    tokens, lengths, group_perm, page_table, k_pool, v_pool, gain_in, qkv_weight, qkv_bias,
    o_weight, gain_mid, gate_weight, up_weight, down_weight,
):
    half = HEAD_DIM // 2
    inverse = np.exp(-np.arange(half) * (2.0 / HEAD_DIM) * np.log(ROPE_BASE)).astype(np.float32)
    inverse = jnp.asarray(np.concatenate([inverse, inverse]))
    position = (lengths[:, None] + jnp.arange(STEPS, dtype=jnp.int32)[None, :]).astype(F32)
    angle = position[..., None] * inverse
    cosine = jnp.cos(angle)
    sine = jnp.where(jnp.arange(HEAD_DIM) < half, -1.0, 1.0) * jnp.sin(angle)

    send, xt, hot = call(
        start_kernel,
        [sds((N_SEQ, FEAT_PAD, ROWS)), sds((FEAT, ROWS), F32), sds((ROWS, ROWS))],
        group_perm, tokens.reshape(ROWS, FEAT), gain_in[None, :],
        anys=(0, 1, 2),
        scratch=[
            pltpu.SMEM((REQUESTS,), jnp.int32),
            pltpu.VMEM((ROWS, FEAT), BF),
            pltpu.VMEM((1, FEAT), F32),
            pltpu.SemaphoreType.DMA((3,)),
        ],
    )
    got = exchange(send, "seq")
    send = call(
        qkv_kernel, sds((N_GRP, GROUP_ROWS, QPAD)), got, qkv_weight,
        scratch=[pltpu.VMEM((GFEAT, ROWS), F32)],
    )
    got = exchange(send, "grp")
    bias = jnp.pad(qkv_bias, (0, QPAD - QCOLS))[None, :]
    send = call(qkv_sum_kernel, sds((N_SEQ, GROUP_ROWS, QPAD)), got, bias)
    got = exchange(send, "seq")
    send = call(
        attend_kernel, sds((N_SEQ, GROUP_ROWS, 4 * HEAD_DIM)),
        group_perm, lengths, page_table, got, cosine, sine, k_pool, v_pool,
        smem=(0, 1, 2), anys=(6, 7),
        scratch=[
            pltpu.VMEM((REQ_GRP, KV_HEADS * QROWS, 2 * HEAD_DIM), F32),
            pltpu.VMEM((PAGE, KV_HEADS * HEAD_DIM), BF),
            pltpu.VMEM((PAGE, KV_HEADS * HEAD_DIM), BF),
            pltpu.VMEM((2, GROUP_ROWS, HEAD_DIM), F32),
            pltpu.VMEM((KV_HEADS * QROWS, SHARD_KEYS + PAGE), F32),
            pltpu.VMEM((N_SEQ, GROUP_ROWS, 4 * HEAD_DIM), F32),
            pltpu.VMEM((REQ_GRP, SHARD_KEYS, KV_HEADS * HEAD_DIM), BF),
            pltpu.VMEM((REQ_GRP, SHARD_KEYS, KV_HEADS * HEAD_DIM), BF),
            pltpu.SemaphoreType.DMA((2, REQ_GRP)),
        ],
    )
    got = exchange(send, "seq")
    send = call(merge_kernel, sds((N_GRP, GROUP_ROWS, 3 * HEAD_DIM)), got)
    got = exchange(send, "grp")
    send = call(project_kernel, sds((N_SEQ, FEAT, ROWS)), got, o_weight)
    got = exchange(send, "seq")
    send, res = call(
        middle_kernel, [sds((N_SEQ, FEAT_PAD, ROWS)), sds((FEAT, ROWS), F32)],
        got, xt, gain_mid[:, None],
    )
    got = exchange(send, "seq")
    keep, give = call(
        gate_kernel,
        [sds((N_CHIP, GROUP_ROWS, 2 * FPAD), F32), sds((N_CHIP, GROUP_ROWS, 2 * FPAD))],
        got, gate_weight, up_weight,
        scratch=[pltpu.VMEM((GFEAT, ROWS), F32)],
    )
    send = call(pair_kernel, sds((N_CHIP, GROUP_ROWS, 2 * FPAD)), keep, swap_cores(give))
    got = exchange_chips(send)
    send = call(hidden_kernel, sds((N_GRP, GROUP_ROWS, FPAD)), got)
    got = exchange(send, "grp")
    send = call(project_kernel, sds((N_SEQ, FEAT, ROWS)), got, down_weight)
    got = exchange(send, "seq")
    out = call(finish_kernel, sds((ROWS, FEAT)), got, res, hot)
    return out.reshape(REQUESTS, STEPS, FEAT)


def solution(mesh):
    return jax.shard_map(
        body,
        mesh=mesh,
        in_specs=(
            P(None, None, ("grp", "seq")),
            P(),
            P(),
            P(),
            P(("grp", "seq"), None, None),
            P(("grp", "seq"), None, None),
            P(("grp", "seq")),
            P("grp", "seq"),
            P("seq"),
            P("seq", "grp"),
            P(("grp", "seq")),
            P("grp", "seq"),
            P("grp", "seq"),
            P("seq", "grp"),
        ),
        out_specs=P(None, None, ("grp", "seq")),
        check_vma=False,
    )
```

```python
import functools

import jax
import jax.numpy as jnp
import numpy as np
from jax import lax
from jax.experimental import pallas as pl
from jax.experimental.pallas import tpu as pltpu
from jax.sharding import PartitionSpec as P

D = 5120
HEADS = 40
KV_HEADS = 8
HEAD_DIM = 128
STEPS = 4
REQ_GRP = 4
SHARD_PAGES = 8
PAGE = 128
REQUESTS = 32
ROWS = REQUESTS * STEPS
GROUP_ROWS = REQ_GRP * STEPS
N_GRP = 8
N_SEQ = 16
N_CHIP = N_GRP // 2
FEAT = D // (N_GRP * N_SEQ)
FEAT_PAD = 48
GFEAT = D // N_GRP
QCOLS = 448
QPAD = 512
OCOLS = 320
FCOLS = 864
FPAD = 896
QROWS = 24
SHARD_KEYS = SHARD_PAGES * PAGE
EPSILON = 1e-06
LOW_SCORE = -1e30
ROPE_BASE = 1000000.0
BF = jnp.bfloat16
COVER = pl.CostEstimate(flops=10**10, transcendentals=0, bytes_accessed=64 << 20)
NT = (((1,), (1,)), ((), ()))
F32 = jnp.float32


def call(kernel, outs, *args, smem=(), anys=(), scratch=(), cost=None):
    specs = []
    for i in range(len(args)):
        if i in smem:
            specs.append(pl.BlockSpec(memory_space=pltpu.SMEM))
        elif i in anys:
            specs.append(pl.BlockSpec(memory_space=pltpu.HBM))
        else:
            specs.append(pl.BlockSpec(memory_space=pltpu.VMEM))
    args = [pltpu.with_memory_space_constraint(v, pltpu.HBM) if i in anys else v for i, v in enumerate(args)]
    many = isinstance(outs, (list, tuple))
    vm = pl.BlockSpec(memory_space=pltpu.VMEM)
    return pl.pallas_call(
        kernel,
        out_shape=outs,
        in_specs=specs,
        out_specs=[vm] * len(outs) if many else vm,
        scratch_shapes=list(scratch),
        name=getattr(kernel, "__name__", "kernel"),
        cost_estimate=cost,
        compiler_params=pltpu.CompilerParams(vmem_limit_bytes=16 << 20),
    )(*args)


def sds(shape, dtype=BF):
    return jax.ShapeDtypeStruct(shape, dtype)


def split(value):
    hi = value.astype(BF).astype(F32)
    return hi, value - hi


def iota(shape, axis):
    return lax.broadcasted_iota(jnp.int32, shape, axis)


def spread_features(value, squares, out_ref):
    hi, lo = split(squares)
    tail = jnp.where(iota((8, ROWS), 0) == 0, hi, jnp.where(iota((8, ROWS), 0) == 1, lo, 0.0))
    block = jnp.concatenate([value, tail], axis=0).astype(BF)
    for s in range(N_SEQ):
        out_ref[s] = block


def start_kernel(perm_hbm, tok_hbm, gain_hbm, send_ref, xt_ref, hot_ref, perm_ref, tok_ref, gain_ref, sems):
    copies = [
        pltpu.make_async_copy(perm_hbm, perm_ref, sems.at[0]),
        pltpu.make_async_copy(tok_hbm, tok_ref, sems.at[1]),
        pltpu.make_async_copy(gain_hbm, gain_ref, sems.at[2]),
    ]
    for copy in copies:
        copy.start()
    for copy in copies:
        copy.wait()
    lane = iota((8, ROWS), 1)
    source = lane & (STEPS - 1)
    for n in range(REQUESTS):
        source = source + jnp.where((lane >> 2) == n, perm_ref[n] * STEPS, 0)
    hot = jnp.where(iota((ROWS, ROWS), 0) == source[0:1, :], 1.0, 0.0).astype(BF)
    hot_ref[...] = hot
    tok = tok_ref[...]
    scaled = (tok.astype(F32) * gain_ref[...]).astype(BF)
    turn = (((0,), (0,)), ((), ()))
    xt = lax.dot_general(tok, hot, turn, preferred_element_type=F32)
    xt_ref[...] = xt
    squares = jnp.sum(xt * xt, axis=0, keepdims=True)
    spread_features(lax.dot_general(scaled, hot, turn, preferred_element_type=F32), squares, send_ref)


def collect_features(in_ref, scratch):
    squares = jnp.zeros((1, ROWS), F32)
    for s in range(N_SEQ):
        block = in_ref[s].astype(F32)
        scratch[s * FEAT : (s + 1) * FEAT, :] = block[:FEAT]
        squares = squares + block[FEAT : FEAT + 1] + block[FEAT + 1 : FEAT + 2]
    value = scratch[...].T.astype(BF)
    squares = jnp.broadcast_to(squares, (ROWS, ROWS)).T
    return value, squares


def qkv_kernel(in_ref, w_ref, cos_ref, sin_ref, gain_ref, bias_ref, out_ref, scratch):
    value, squares = collect_features(in_ref, scratch)
    part = lax.dot_general(value, w_ref[...], NT, preferred_element_type=F32)
    hi, lo = split(squares)
    for g in range(N_GRP):
        rows = slice(g * GROUP_ROWS, (g + 1) * GROUP_ROWS)
        out_ref[g, :, :QCOLS] = part[rows].astype(BF)
        out_ref[g, :, QCOLS:] = jnp.where(
            iota((GROUP_ROWS, QPAD - QCOLS), 1) < 32, hi[rows, : QPAD - QCOLS], lo[rows, : QPAD - QCOLS]
        ).astype(BF)


def scale_of(total, at):
    squares = total[:, at : at + 1] + total[:, at + 16 : at + 17]
    return lax.rsqrt(squares / D + EPSILON)


def qkv_sum_kernel(in_ref, bias_ref, out_ref):
    total = in_ref[0].astype(F32)
    for g in range(1, N_GRP):
        total = total + in_ref[g].astype(F32)
    squares = total[:, QCOLS : QCOLS + 1] + total[:, QCOLS + 32 : QCOLS + 33]
    scale = lax.rsqrt(squares / D + EPSILON)
    value = total * scale + bias_ref[...]
    value = jnp.where(iota(value.shape, 1) < QCOLS, value, 0.0)
    odd = lax.rem(lax.axis_index("seq"), 2) == 1
    value = jnp.where(odd, pltpu.roll(value, QPAD - QCOLS, 1), value).astype(BF)
    for s in range(N_SEQ):
        out_ref[s] = value


def attend_kernel(
    perm_ref, len_ref, page_ref, in_ref, cos_ref, sin_ref, k_ref, v_ref, out_ref,
    qbuf, knew, vnew, rot, sbuf, obuf,
):
    grp_idx = lax.axis_index("grp")
    seq_idx = lax.axis_index("seq")
    members = [perm_ref[grp_idx * REQ_GRP + r] for r in range(REQ_GRP)]
    for r in range(REQ_GRP):
        rot[0, r * STEPS : (r + 1) * STEPS, :] = cos_ref[members[r]]
        rot[1, r * STEPS : (r + 1) * STEPS, :] = sin_ref[members[r]]
    cosine = rot[0]
    sine = rot[1]
    knew[...] = jnp.zeros_like(knew)
    vnew[...] = jnp.zeros_like(vnew)
    qbuf[...] = jnp.zeros_like(qbuf)
    for pair in range(N_SEQ // 2):
        even = in_ref[2 * pair].astype(F32)
        odd = in_ref[2 * pair + 1].astype(F32)
        for k in range(7):
            lanes = slice(k * 128, (k + 1) * 128)
            olanes = slice((k - 3) * 128, (k - 2) * 128)
            if k < 3:
                value = even[:, lanes]
            elif k == 3:
                value = even[:, lanes] + odd[:, olanes]
            else:
                value = odd[:, olanes]
            head = pair * 7 + k
            if head < HEADS + KV_HEADS:
                value = value * cosine + pltpu.roll(value, HEAD_DIM // 2, 1) * sine
            if head < HEADS:
                h, j = divmod(head, HEADS // KV_HEADS)
                for r in range(REQ_GRP):
                    at = h * QROWS + j * STEPS
                    side = (h % 2) * HEAD_DIM
                    qbuf[r, at : at + STEPS, side : side + HEAD_DIM] = value[r * STEPS : (r + 1) * STEPS]
            elif head < HEADS + KV_HEADS:
                h = head - HEADS
                knew[:GROUP_ROWS, h * HEAD_DIM : (h + 1) * HEAD_DIM] = value.astype(BF)
            else:
                h = head - HEADS - KV_HEADS
                vnew[:GROUP_ROWS, h * HEAD_DIM : (h + 1) * HEAD_DIM] = value.astype(BF)

    score_scale = HEAD_DIM ** (-0.5)
    power = score_scale * float(np.log2(np.e))
    step = iota((2 * QROWS, PAGE), 0) & (STEPS - 1)
    column = iota((2 * QROWS, PAGE), 1)
    own_live = ((column & (STEPS - 1)) <= step) & (seq_idx == N_SEQ - 1) & (column < GROUP_ROWS)
    place = iota((8, SHARD_KEYS), 1)
    group = iota((2 * QROWS, HEAD_DIM), 1) >> 3
    word = lax.rem(group, 3)
    part_lane = iota((STEPS, HEAD_DIM), 1)
    for r in range(REQ_GRP):
        slots = [page_ref[members[r], seq_idx * SHARD_PAGES + p] for p in range(SHARD_PAGES)]
        live = len_ref[members[r]] - seq_idx * SHARD_KEYS
        bias = jnp.where(place < live, 0.0, LOW_SCORE)[0:1]
        own_bias = jnp.where(own_live & ((column >> 2) == r), 0.0, LOW_SCORE)
        for h in range(0, KV_HEADS, 2):
            lanes = slice(h * HEAD_DIM, (h + 2) * HEAD_DIM)
            rows = slice(h * QROWS, (h + 2) * QROWS)
            query = qbuf[r, rows, :].astype(BF)
            keys = jnp.concatenate([k_ref[slot, :, lanes] for slot in slots], axis=0)
            scores = lax.dot_general(query, keys, NT, preferred_element_type=F32)
            sbuf[rows, :SHARD_KEYS] = scores + bias
            own = lax.dot_general(query, knew[:, lanes], NT, preferred_element_type=F32)
            sbuf[rows, SHARD_KEYS:] = own + own_bias
        for pair in range(0, KV_HEADS, 2):
            lanes = slice(pair * HEAD_DIM, (pair + 2) * HEAD_DIM)
            scores = sbuf[pair * QROWS : (pair + 2) * QROWS, :]
            best = jnp.max(scores, axis=1, keepdims=True)
            weight = jnp.exp2((scores - best) * power)
            total = jnp.sum(weight, axis=1, keepdims=True)
            weight = weight.astype(BF)
            values = jnp.concatenate([v_ref[slot, :, lanes] for slot in slots], axis=0)
            both = jnp.dot(
                weight[:, :SHARD_KEYS], values, preferred_element_type=F32
            ) + jnp.dot(weight[:, SHARD_KEYS:], vnew[:, lanes], preferred_element_type=F32)
            both = both / total
            levels = jnp.where(best > 0.1 * LOW_SCORE, best * score_scale + jnp.log(total), LOW_SCORE)
            hi, rest = split(levels)
            mid, low = split(rest)
            levels = jnp.where(word == 0, hi, jnp.where(word == 1, mid, low))
            for side in range(2):
                h = pair + side
                mixed = both[side * QROWS : (side + 1) * QROWS, side * HEAD_DIM : (side + 1) * HEAD_DIM]
                level = levels[side * QROWS : (side + 1) * QROWS]
                for half in range(2):
                    to = slice(r * STEPS, (r + 1) * STEPS)
                    parts = [slice((2 * half + j) * STEPS, (2 * half + j + 1) * STEPS) for j in range(3)]
                    for j in range(3):
                        obuf[2 * h + half, to, j * HEAD_DIM : (j + 1) * HEAD_DIM] = mixed[parts[j]]
                    obuf[2 * h + half, to, 3 * HEAD_DIM :] = jnp.where(
                        part_lane < 24, level[parts[0]], jnp.where(part_lane < 48, level[parts[1]], level[parts[2]])
                    )
    for s in range(N_SEQ):
        out_ref[s] = obuf[s].astype(BF)


def merge_kernel(in_ref, out_ref):
    levels = []
    for s in range(N_SEQ):
        cols = in_ref[s, :, 3 * HEAD_DIM :].astype(F32)
        levels.append(
            [cols[:, a : a + 1] + cols[:, a + 8 : a + 9] + cols[:, a + 16 : a + 17] for a in (0, 24, 48)]
        )
    out = []
    for j in range(3):
        best = functools.reduce(jnp.maximum, [level[j] for level in levels])
        total = jnp.zeros_like(best)
        value = jnp.zeros((GROUP_ROWS, HEAD_DIM), F32)
        for s in range(N_SEQ):
            factor = jnp.exp(levels[s][j] - best)
            total = total + factor
            value = value + in_ref[s, :, j * HEAD_DIM : (j + 1) * HEAD_DIM].astype(F32) * factor
        out.append(value / total)
    value = jnp.concatenate(out, axis=1)
    odd = lax.rem(lax.axis_index("seq"), 2) == 1
    value = jnp.where(odd, pltpu.roll(value, 3 * HEAD_DIM - HEAD_DIM // 2, 1), value).astype(BF)
    for g in range(N_GRP):
        out_ref[g] = value


def send_back(part, out_ref):
    turned = part.T
    for s in range(N_SEQ):
        out_ref[s] = turned[s * FEAT : (s + 1) * FEAT].astype(BF)


def on_second_core():
    return lax.rem(lax.axis_index("grp"), 2) == 1


def on_second_core():
    return lax.rem(lax.axis_index("grp"), 2) == 1


def project_kernel(in_ref, w_ref, out_ref):
    value = in_ref[...].reshape(ROWS, in_ref.shape[2])[:, : w_ref.shape[0]]
    send_back(jnp.dot(value, w_ref[...], preferred_element_type=F32), out_ref)


def middle_kernel(in_ref, xt_ref, gain_ref, send_ref, res_ref):
    total = xt_ref[...]
    part = in_ref[0].astype(F32)
    for s in range(1, N_SEQ):
        part = part + in_ref[s].astype(F32)
    total = total + part
    res_ref[...] = total
    squares = jnp.sum(total * total, axis=0, keepdims=True)
    spread_features(total * gain_ref[...], squares, send_ref)


def gate_kernel(in_ref, gate_ref, up_ref, keep_ref, give_ref, scratch):
    value, squares = collect_features(in_ref, scratch)
    gate = lax.dot_general(value, gate_ref[...], NT, preferred_element_type=F32)
    up = lax.dot_general(value, up_ref[...], NT, preferred_element_type=F32)
    hi, lo = split(squares)
    tail = FPAD - FCOLS
    sums = jnp.where(iota((ROWS, tail), 1) < tail // 2, hi[:, :tail], lo[:, :tail])
    second = on_second_core()
    spare = slice(FCOLS, FPAD)
    for x in range(N_CHIP):
        first_rows = slice(2 * x * GROUP_ROWS, (2 * x + 1) * GROUP_ROWS)
        last_rows = slice((2 * x + 1) * GROUP_ROWS, (2 * x + 2) * GROUP_ROWS)
        for lanes, part in (
            (slice(0, FCOLS), gate),
            (spare, sums),
            (slice(FPAD, FPAD + FCOLS), up),
        ):
            first = part[first_rows]
            last = part[last_rows]
            keep_ref[x, :, lanes] = jnp.where(second, last, first)
            give_ref[x, :, lanes] = jnp.where(second, first, last).astype(BF)
        keep_ref[x, :, FPAD + FCOLS :] = jnp.zeros((GROUP_ROWS, tail), F32)
        give_ref[x, :, FPAD + FCOLS :] = jnp.zeros((GROUP_ROWS, tail), BF)


def pair_kernel(keep_ref, got_ref, out_ref):
    tail = (FPAD - FCOLS) // 2
    start = FPAD - 128
    lane = iota((GROUP_ROWS, 128), 1)
    for x in range(N_CHIP):
        total = keep_ref[x] + got_ref[x].astype(F32)
        out_ref[x] = total.astype(BF)
        last = total[:, start:FPAD]
        hi, lo = split(last + pltpu.roll(last, 128 - tail, 1))
        last = jnp.where(
            lane < 128 - 2 * tail, last, jnp.where(lane < 128 - tail, hi, pltpu.roll(lo, tail, 1))
        )
        out_ref[x, :, start:FPAD] = last.astype(BF)


def hidden_kernel(in_ref, out_ref):
    total = in_ref[0].astype(F32)
    for x in range(1, N_CHIP):
        total = total + in_ref[x].astype(F32)
    scale = scale_of(total, FCOLS)
    gate = total[:, :FPAD] * scale
    up = total[:, FPAD:] * scale
    value = (gate / (1.0 + jnp.exp(-gate)) * up).astype(BF)
    for g in range(N_GRP):
        out_ref[g] = value


def finish_kernel(in_ref, res_ref, hot_ref, out_ref):
    part = in_ref[0].astype(F32)
    for s in range(1, N_SEQ):
        part = part + in_ref[s].astype(F32)
    total = (res_ref[...] + part).astype(BF)
    out_ref[...] = lax.dot_general(
        hot_ref[...], total, (((1,), (1,)), ((), ())), preferred_element_type=F32
    ).astype(BF)


def exchange(value, axis):
    return lax.all_to_all(value, axis, 0, 0, tiled=False)


def exchange_chips(value):
    groups = [list(range(core, N_GRP, 2)) for core in range(2)]
    return lax.all_to_all(value, "grp", 0, 0, axis_index_groups=groups, tiled=False)


def swap_cores(value):
    return lax.ppermute(value, "grp", [(i, i ^ 1) for i in range(N_GRP)])


def body(
    tokens, lengths, group_perm, page_table, k_pool, v_pool, gain_in, qkv_weight, qkv_bias,
    o_weight, gain_mid, gate_weight, up_weight, down_weight,
):
    half = HEAD_DIM // 2
    inverse = np.exp(-np.arange(half) * (2.0 / HEAD_DIM) * np.log(ROPE_BASE)).astype(np.float32)
    inverse = jnp.asarray(np.concatenate([inverse, inverse]))
    position = (lengths[:, None] + jnp.arange(STEPS, dtype=jnp.int32)[None, :]).astype(F32)
    angle = position[..., None] * inverse
    cosine = jnp.cos(angle)
    sine = jnp.where(jnp.arange(HEAD_DIM) < half, -1.0, 1.0) * jnp.sin(angle)

    send, xt, hot = call(
        start_kernel,
        [sds((N_SEQ, FEAT_PAD, ROWS)), sds((FEAT, ROWS), F32), sds((ROWS, ROWS))],
        group_perm, tokens.reshape(ROWS, FEAT), gain_in[None, :],
        anys=(0, 1, 2),
        scratch=[
            pltpu.SMEM((REQUESTS,), jnp.int32),
            pltpu.VMEM((ROWS, FEAT), BF),
            pltpu.VMEM((1, FEAT), F32),
            pltpu.SemaphoreType.DMA((3,)),
        ],
        cost=COVER,
    )
    got = exchange(send, "seq")
    bias = jnp.pad(qkv_bias, (0, QPAD - QCOLS))[None, :]
    gain = gain_mid[:, None]
    send = call(
        qkv_kernel, sds((N_GRP, GROUP_ROWS, QPAD)), got, qkv_weight.T, cosine, sine, gain, bias,
        scratch=[pltpu.VMEM((GFEAT, ROWS), F32)], cost=COVER,
    )
    got = exchange(send, "grp")
    send = call(qkv_sum_kernel, sds((N_SEQ, GROUP_ROWS, QPAD)), got, bias, cost=COVER)
    got = exchange(send, "seq")
    send = call(
        attend_kernel, sds((N_SEQ, GROUP_ROWS, 4 * HEAD_DIM)),
        group_perm, lengths, page_table, got, cosine, sine, k_pool, v_pool,
        smem=(0, 1, 2),
        scratch=[
            pltpu.VMEM((REQ_GRP, KV_HEADS * QROWS, 2 * HEAD_DIM), F32),
            pltpu.VMEM((PAGE, KV_HEADS * HEAD_DIM), BF),
            pltpu.VMEM((PAGE, KV_HEADS * HEAD_DIM), BF),
            pltpu.VMEM((2, GROUP_ROWS, HEAD_DIM), F32),
            pltpu.VMEM((KV_HEADS * QROWS, SHARD_KEYS + PAGE), F32),
            pltpu.VMEM((N_SEQ, GROUP_ROWS, 4 * HEAD_DIM), F32),
        ],
    )
    got = exchange(send, "seq")
    send = call(merge_kernel, sds((N_GRP, GROUP_ROWS, 3 * HEAD_DIM)), got)
    got = exchange(send, "grp")
    send = call(project_kernel, sds((N_SEQ, FEAT, ROWS)), got, o_weight)
    got = exchange(send, "seq")
    send, res = call(
        middle_kernel, [sds((N_SEQ, FEAT_PAD, ROWS)), sds((FEAT, ROWS), F32)],
        got, xt, gain,
    )
    got = exchange(send, "seq")
    keep, give = call(
        gate_kernel,
        [sds((N_CHIP, GROUP_ROWS, 2 * FPAD), F32), sds((N_CHIP, GROUP_ROWS, 2 * FPAD))],
        got, gate_weight.T, up_weight.T,
        scratch=[pltpu.VMEM((GFEAT, ROWS), F32)],
    )
    send = call(pair_kernel, sds((N_CHIP, GROUP_ROWS, 2 * FPAD)), keep, swap_cores(give))
    got = exchange_chips(send)
    send = call(hidden_kernel, sds((N_GRP, GROUP_ROWS, FPAD)), got)
    got = exchange(send, "grp")
    send = call(project_kernel, sds((N_SEQ, FEAT, ROWS)), got, down_weight)
    got = exchange(send, "seq")
    out = call(finish_kernel, sds((ROWS, FEAT)), got, res, hot)
    return out.reshape(REQUESTS, STEPS, FEAT)


def solution(mesh):
    return jax.shard_map(
        body,
        mesh=mesh,
        in_specs=(
            P(None, None, ("grp", "seq")),
            P(),
            P(),
            P(),
            P(("grp", "seq"), None, None),
            P(("grp", "seq"), None, None),
            P(("grp", "seq")),
            P("grp", "seq"),
            P("seq"),
            P("seq", "grp"),
            P(("grp", "seq")),
            P("grp", "seq"),
            P("grp", "seq"),
            P("seq", "grp"),
        ),
        out_specs=P(None, None, ("grp", "seq")),
        check_vma=False,
    )
```

```python
import functools

import jax
import jax.numpy as jnp
import numpy as np
from jax import lax
from jax.experimental import pallas as pl
from jax.experimental.pallas import tpu as pltpu
from jax.sharding import PartitionSpec as P

D = 5120
HEADS = 40
KV_HEADS = 8
HEAD_DIM = 128
STEPS = 4
REQ_GRP = 4
SHARD_PAGES = 8
PAGE = 128
REQUESTS = 32
ROWS = REQUESTS * STEPS
GROUP_ROWS = REQ_GRP * STEPS
N_GRP = 8
N_SEQ = 16
N_CHIP = N_GRP // 2
FEAT = D // (N_GRP * N_SEQ)
FEAT_PAD = 48
GFEAT = D // N_GRP
QCOLS = 448
QPAD = 512
OCOLS = 320
FCOLS = 864
FPAD = 896
QROWS = 24
SHARD_KEYS = SHARD_PAGES * PAGE
EPSILON = 1e-06
LOW_SCORE = -1e30
ROPE_BASE = 1000000.0
BF = jnp.bfloat16
COVER = pl.CostEstimate(flops=10**10, transcendentals=0, bytes_accessed=64 << 20)
NT = (((1,), (1,)), ((), ()))
F32 = jnp.float32


def call(kernel, outs, *args, smem=(), anys=(), scratch=(), cost=None):
    specs = []
    for i in range(len(args)):
        if i in smem:
            specs.append(pl.BlockSpec(memory_space=pltpu.SMEM))
        elif i in anys:
            specs.append(pl.BlockSpec(memory_space=pltpu.HBM))
        else:
            specs.append(pl.BlockSpec(memory_space=pltpu.VMEM))
    args = [pltpu.with_memory_space_constraint(v, pltpu.HBM) if i in anys else v for i, v in enumerate(args)]
    many = isinstance(outs, (list, tuple))
    vm = pl.BlockSpec(memory_space=pltpu.VMEM)
    return pl.pallas_call(
        kernel,
        out_shape=outs,
        in_specs=specs,
        out_specs=[vm] * len(outs) if many else vm,
        scratch_shapes=list(scratch),
        name=getattr(kernel, "__name__", "kernel"),
        cost_estimate=cost,
        compiler_params=pltpu.CompilerParams(vmem_limit_bytes=16 << 20),
    )(*args)


def sds(shape, dtype=BF):
    return jax.ShapeDtypeStruct(shape, dtype)


def split(value):
    hi = value.astype(BF).astype(F32)
    return hi, value - hi


def iota(shape, axis):
    return lax.broadcasted_iota(jnp.int32, shape, axis)


def spread_features(value, squares, out_ref):
    hi, lo = split(squares)
    tail = jnp.where(iota((8, ROWS), 0) == 0, hi, jnp.where(iota((8, ROWS), 0) == 1, lo, 0.0))
    block = jnp.concatenate([value, tail], axis=0).astype(BF)
    for s in range(N_SEQ):
        out_ref[s] = block


def start_kernel(perm_hbm, tok_hbm, gain_hbm, send_ref, xt_ref, hot_ref, perm_ref, tok_ref, gain_ref, sems):
    copies = [
        pltpu.make_async_copy(perm_hbm, perm_ref, sems.at[0]),
        pltpu.make_async_copy(tok_hbm, tok_ref, sems.at[1]),
        pltpu.make_async_copy(gain_hbm, gain_ref, sems.at[2]),
    ]
    for copy in copies:
        copy.start()
    for copy in copies:
        copy.wait()
    lane = iota((8, ROWS), 1)
    source = lane & (STEPS - 1)
    for n in range(REQUESTS):
        source = source + jnp.where((lane >> 2) == n, perm_ref[n] * STEPS, 0)
    hot = jnp.where(iota((ROWS, ROWS), 0) == source[0:1, :], 1.0, 0.0).astype(BF)
    hot_ref[...] = hot
    tok = tok_ref[...]
    scaled = (tok.astype(F32) * gain_ref[...]).astype(BF)
    turn = (((0,), (0,)), ((), ()))
    xt = lax.dot_general(tok, hot, turn, preferred_element_type=F32)
    xt_ref[...] = xt
    squares = jnp.sum(xt * xt, axis=0, keepdims=True)
    spread_features(lax.dot_general(scaled, hot, turn, preferred_element_type=F32), squares, send_ref)


def collect_features(in_ref, scratch):
    squares = jnp.zeros((1, ROWS), F32)
    for s in range(N_SEQ):
        block = in_ref[s].astype(F32)
        scratch[s * FEAT : (s + 1) * FEAT, :] = block[:FEAT]
        squares = squares + block[FEAT : FEAT + 1] + block[FEAT + 1 : FEAT + 2]
    value = scratch[...].T.astype(BF)
    squares = jnp.broadcast_to(squares, (ROWS, ROWS)).T
    return value, squares


def qkv_kernel(in_ref, w_ref, out_ref, scratch):
    value, squares = collect_features(in_ref, scratch)
    part = lax.dot_general(value, w_ref[...], NT, preferred_element_type=F32)
    hi, lo = split(squares)
    for g in range(N_GRP):
        rows = slice(g * GROUP_ROWS, (g + 1) * GROUP_ROWS)
        out_ref[g, :, :QCOLS] = part[rows].astype(BF)
        out_ref[g, :, QCOLS:] = jnp.where(
            iota((GROUP_ROWS, QPAD - QCOLS), 1) < 32, hi[rows, : QPAD - QCOLS], lo[rows, : QPAD - QCOLS]
        ).astype(BF)


def scale_of(total, at):
    squares = total[:, at : at + 1] + total[:, at + 16 : at + 17]
    return lax.rsqrt(squares / D + EPSILON)


def qkv_sum_kernel(in_ref, bias_ref, out_ref, scratch):
    scratch[...] = jnp.zeros_like(scratch)
    scratch[:, :QCOLS] = bias_ref[...]
    total = in_ref[0].astype(F32)
    for g in range(1, N_GRP):
        total = total + in_ref[g].astype(F32)
    squares = total[:, QCOLS : QCOLS + 1] + total[:, QCOLS + 32 : QCOLS + 33]
    scale = lax.rsqrt(squares / D + EPSILON)
    value = total * scale + scratch[...]
    value = jnp.where(iota(value.shape, 1) < QCOLS, value, 0.0)
    odd = lax.rem(lax.axis_index("seq"), 2) == 1
    value = jnp.where(odd, pltpu.roll(value, QPAD - QCOLS, 1), value).astype(BF)
    for s in range(N_SEQ):
        out_ref[s] = value


def cos_sin(angle):
    turns = jnp.floor(angle * float(2.0 / np.pi) + 0.5)
    rest = ((angle - turns * 1.5703125) - turns * 4.837512969970703125e-4) - turns * 7.54978995489188216e-8
    square = rest * rest
    sine = ((-1.9515295891e-4 * square + 8.3321608736e-3) * square - 1.6666654611e-1) * square * rest + rest
    cosine = (
        (2.443315711809948e-5 * square - 1.388731625493765e-3) * square + 4.166664568298827e-2
    ) * square * square - 0.5 * square + 1.0
    quadrant = turns.astype(jnp.int32) & 3
    odd = (quadrant & 1) == 1
    first = jnp.where(odd, sine, cosine)
    second = jnp.where(odd, cosine, sine)
    return (
        jnp.where((quadrant == 1) | (quadrant == 2), -first, first),
        jnp.where(quadrant >= 2, -second, second),
    )


def attend_kernel(
    perm_ref, len_ref, page_ref, in_ref, inverse_ref, k_ref, v_ref, out_ref,
    qbuf, knew, vnew, sbuf, obuf,
):
    grp_idx = lax.axis_index("grp")
    seq_idx = lax.axis_index("seq")
    members = [perm_ref[grp_idx * REQ_GRP + r] for r in range(REQ_GRP)]
    row = iota((GROUP_ROWS, HEAD_DIM), 0)
    position = row & (STEPS - 1)
    for r in range(REQ_GRP):
        position = position + jnp.where((row >> 2) == r, len_ref[members[r]], 0)
    cosine, sine = cos_sin(position.astype(F32) * inverse_ref[...])
    sine = jnp.where(iota(sine.shape, 1) < HEAD_DIM // 2, -sine, sine)
    knew[...] = jnp.zeros_like(knew)
    vnew[...] = jnp.zeros_like(vnew)
    qbuf[...] = jnp.zeros_like(qbuf)
    for pair in range(N_SEQ // 2):
        even = in_ref[2 * pair].astype(F32)
        odd = in_ref[2 * pair + 1].astype(F32)
        for k in range(7):
            lanes = slice(k * 128, (k + 1) * 128)
            olanes = slice((k - 3) * 128, (k - 2) * 128)
            if k < 3:
                value = even[:, lanes]
            elif k == 3:
                value = even[:, lanes] + odd[:, olanes]
            else:
                value = odd[:, olanes]
            head = pair * 7 + k
            if head < HEADS + KV_HEADS:
                value = value * cosine + pltpu.roll(value, HEAD_DIM // 2, 1) * sine
            if head < HEADS:
                h, j = divmod(head, HEADS // KV_HEADS)
                for r in range(REQ_GRP):
                    at = h * QROWS + j * STEPS
                    side = (h % 2) * HEAD_DIM
                    qbuf[r, at : at + STEPS, side : side + HEAD_DIM] = value[r * STEPS : (r + 1) * STEPS]
            elif head < HEADS + KV_HEADS:
                h = head - HEADS
                knew[:GROUP_ROWS, h * HEAD_DIM : (h + 1) * HEAD_DIM] = value.astype(BF)
            else:
                h = head - HEADS - KV_HEADS
                vnew[:GROUP_ROWS, h * HEAD_DIM : (h + 1) * HEAD_DIM] = value.astype(BF)

    score_scale = HEAD_DIM ** (-0.5)
    power = score_scale * float(np.log2(np.e))
    step = iota((2 * QROWS, PAGE), 0) & (STEPS - 1)
    column = iota((2 * QROWS, PAGE), 1)
    own_live = ((column & (STEPS - 1)) <= step) & (seq_idx == N_SEQ - 1) & (column < GROUP_ROWS)
    place = iota((8, SHARD_KEYS), 1)
    group = iota((2 * QROWS, HEAD_DIM), 1) >> 3
    word = lax.rem(group, 3)
    part_lane = iota((STEPS, HEAD_DIM), 1)
    for r in range(REQ_GRP):
        slots = [page_ref[members[r], seq_idx * SHARD_PAGES + p] for p in range(SHARD_PAGES)]
        live = len_ref[members[r]] - seq_idx * SHARD_KEYS
        bias = jnp.where(place < live, 0.0, LOW_SCORE)[0:1]
        own_bias = jnp.where(own_live & ((column >> 2) == r), 0.0, LOW_SCORE)
        for h in range(0, KV_HEADS, 2):
            lanes = slice(h * HEAD_DIM, (h + 2) * HEAD_DIM)
            rows = slice(h * QROWS, (h + 2) * QROWS)
            query = qbuf[r, rows, :].astype(BF)
            keys = jnp.concatenate([k_ref[slot, :, lanes] for slot in slots], axis=0)
            scores = lax.dot_general(query, keys, NT, preferred_element_type=F32)
            sbuf[rows, :SHARD_KEYS] = scores + bias
            own = lax.dot_general(query, knew[:, lanes], NT, preferred_element_type=F32)
            sbuf[rows, SHARD_KEYS:] = own + own_bias
        for pair in range(0, KV_HEADS, 2):
            lanes = slice(pair * HEAD_DIM, (pair + 2) * HEAD_DIM)
            scores = sbuf[pair * QROWS : (pair + 2) * QROWS, :]
            best = jnp.max(scores, axis=1, keepdims=True)
            weight = jnp.exp2((scores - best) * power)
            total = jnp.sum(weight, axis=1, keepdims=True)
            weight = weight.astype(BF)
            values = jnp.concatenate([v_ref[slot, :, lanes] for slot in slots], axis=0)
            both = jnp.dot(
                weight[:, :SHARD_KEYS], values, preferred_element_type=F32
            ) + jnp.dot(weight[:, SHARD_KEYS:], vnew[:, lanes], preferred_element_type=F32)
            both = both / total
            levels = jnp.where(best > 0.1 * LOW_SCORE, best * score_scale + jnp.log(total), LOW_SCORE)
            hi, rest = split(levels)
            mid, low = split(rest)
            levels = jnp.where(word == 0, hi, jnp.where(word == 1, mid, low))
            for side in range(2):
                h = pair + side
                mixed = both[side * QROWS : (side + 1) * QROWS, side * HEAD_DIM : (side + 1) * HEAD_DIM]
                level = levels[side * QROWS : (side + 1) * QROWS]
                for half in range(2):
                    to = slice(r * STEPS, (r + 1) * STEPS)
                    parts = [slice((2 * half + j) * STEPS, (2 * half + j + 1) * STEPS) for j in range(3)]
                    for j in range(3):
                        obuf[2 * h + half, to, j * HEAD_DIM : (j + 1) * HEAD_DIM] = mixed[parts[j]]
                    obuf[2 * h + half, to, 3 * HEAD_DIM :] = jnp.where(
                        part_lane < 24, level[parts[0]], jnp.where(part_lane < 48, level[parts[1]], level[parts[2]])
                    )
    for s in range(N_SEQ):
        out_ref[s] = obuf[s].astype(BF)


def merge_kernel(in_ref, out_ref):
    levels = []
    for s in range(N_SEQ):
        cols = in_ref[s, :, 3 * HEAD_DIM :].astype(F32)
        levels.append(
            [cols[:, a : a + 1] + cols[:, a + 8 : a + 9] + cols[:, a + 16 : a + 17] for a in (0, 24, 48)]
        )
    out = []
    for j in range(3):
        best = functools.reduce(jnp.maximum, [level[j] for level in levels])
        total = jnp.zeros_like(best)
        value = jnp.zeros((GROUP_ROWS, HEAD_DIM), F32)
        for s in range(N_SEQ):
            factor = jnp.exp(levels[s][j] - best)
            total = total + factor
            value = value + in_ref[s, :, j * HEAD_DIM : (j + 1) * HEAD_DIM].astype(F32) * factor
        out.append(value / total)
    value = jnp.concatenate(out, axis=1)
    odd = lax.rem(lax.axis_index("seq"), 2) == 1
    value = jnp.where(odd, pltpu.roll(value, 3 * HEAD_DIM - HEAD_DIM // 2, 1), value).astype(BF)
    for g in range(N_GRP):
        out_ref[g] = value


def send_back(part, out_ref):
    turned = part.T
    for s in range(N_SEQ):
        out_ref[s] = turned[s * FEAT : (s + 1) * FEAT].astype(BF)


def on_second_core():
    return lax.rem(lax.axis_index("grp"), 2) == 1


def on_second_core():
    return lax.rem(lax.axis_index("grp"), 2) == 1


def project_kernel(in_ref, w_ref, out_ref):
    value = in_ref[...].reshape(ROWS, in_ref.shape[2])[:, : w_ref.shape[0]]
    send_back(jnp.dot(value, w_ref[...], preferred_element_type=F32), out_ref)


def middle_kernel(in_ref, xt_ref, gain_ref, send_ref, res_ref):
    total = xt_ref[...]
    part = in_ref[0].astype(F32)
    for s in range(1, N_SEQ):
        part = part + in_ref[s].astype(F32)
    total = total + part
    res_ref[...] = total
    squares = jnp.sum(total * total, axis=0, keepdims=True)
    diagonal = iota((FEAT, FEAT), 0) == iota((FEAT, FEAT), 1)
    gain = jnp.sum(jnp.where(diagonal, gain_ref[...], 0.0), axis=1, keepdims=True)
    spread_features(total * gain, squares, send_ref)


def gate_kernel(in_ref, gate_ref, up_ref, keep_ref, give_ref, scratch):
    value, squares = collect_features(in_ref, scratch)
    gate = lax.dot_general(value, gate_ref[...], NT, preferred_element_type=F32)
    up = lax.dot_general(value, up_ref[...], NT, preferred_element_type=F32)
    hi, lo = split(squares)
    tail = FPAD - FCOLS
    sums = jnp.where(iota((ROWS, tail), 1) < tail // 2, hi[:, :tail], lo[:, :tail])
    second = on_second_core()
    spare = slice(FCOLS, FPAD)
    for x in range(N_CHIP):
        first_rows = slice(2 * x * GROUP_ROWS, (2 * x + 1) * GROUP_ROWS)
        last_rows = slice((2 * x + 1) * GROUP_ROWS, (2 * x + 2) * GROUP_ROWS)
        for lanes, part in (
            (slice(0, FCOLS), gate),
            (spare, sums),
            (slice(FPAD, FPAD + FCOLS), up),
        ):
            first = part[first_rows]
            last = part[last_rows]
            keep_ref[x, :, lanes] = jnp.where(second, last, first)
            give_ref[x, :, lanes] = jnp.where(second, first, last).astype(BF)
        keep_ref[x, :, FPAD + FCOLS :] = jnp.zeros((GROUP_ROWS, tail), F32)
        give_ref[x, :, FPAD + FCOLS :] = jnp.zeros((GROUP_ROWS, tail), BF)


def pair_kernel(keep_ref, got_ref, out_ref):
    tail = (FPAD - FCOLS) // 2
    start = FPAD - 128
    lane = iota((GROUP_ROWS, 128), 1)
    for x in range(N_CHIP):
        total = keep_ref[x] + got_ref[x].astype(F32)
        out_ref[x] = total.astype(BF)
        last = total[:, start:FPAD]
        hi, lo = split(last + pltpu.roll(last, 128 - tail, 1))
        last = jnp.where(
            lane < 128 - 2 * tail, last, jnp.where(lane < 128 - tail, hi, pltpu.roll(lo, tail, 1))
        )
        out_ref[x, :, start:FPAD] = last.astype(BF)


def hidden_kernel(in_ref, out_ref):
    total = in_ref[0].astype(F32)
    for x in range(1, N_CHIP):
        total = total + in_ref[x].astype(F32)
    scale = scale_of(total, FCOLS)
    gate = total[:, :FPAD] * scale
    up = total[:, FPAD:] * scale
    value = (gate / (1.0 + jnp.exp(-gate)) * up).astype(BF)
    for g in range(N_GRP):
        out_ref[g] = value


def finish_kernel(in_ref, res_ref, hot_ref, out_ref):
    part = in_ref[0].astype(F32)
    for s in range(1, N_SEQ):
        part = part + in_ref[s].astype(F32)
    total = (res_ref[...] + part).astype(BF)
    out_ref[...] = lax.dot_general(
        hot_ref[...], total, (((1,), (1,)), ((), ())), preferred_element_type=F32
    ).astype(BF)


def exchange(value, axis):
    return lax.all_to_all(value, axis, 0, 0, tiled=False)


def exchange_chips(value):
    groups = [list(range(core, N_GRP, 2)) for core in range(2)]
    return lax.all_to_all(value, "grp", 0, 0, axis_index_groups=groups, tiled=False)


def swap_cores(value):
    return lax.ppermute(value, "grp", [(i, i ^ 1) for i in range(N_GRP)])


def body(
    tokens, lengths, group_perm, page_table, k_pool, v_pool, gain_in, qkv_weight, qkv_bias,
    o_weight, gain_mid, gate_weight, up_weight, down_weight,
):
    half = HEAD_DIM // 2
    inverse = np.exp(-np.arange(half) * (2.0 / HEAD_DIM) * np.log(ROPE_BASE)).astype(np.float32)
    inverse = jnp.asarray(np.concatenate([inverse, inverse]))[None, :]

    send, xt, hot = call(
        start_kernel,
        [sds((N_SEQ, FEAT_PAD, ROWS)), sds((FEAT, ROWS), F32), sds((ROWS, ROWS))],
        group_perm, tokens.reshape(ROWS, FEAT), gain_in[None, :],
        anys=(0, 1, 2),
        scratch=[
            pltpu.SMEM((REQUESTS,), jnp.int32),
            pltpu.VMEM((ROWS, FEAT), BF),
            pltpu.VMEM((1, FEAT), F32),
            pltpu.SemaphoreType.DMA((3,)),
        ],
        cost=COVER,
    )
    got = exchange(send, "seq")
    send = call(
        qkv_kernel, sds((N_GRP, GROUP_ROWS, QPAD)), got, qkv_weight.T,
        scratch=[pltpu.VMEM((GFEAT, ROWS), F32)], cost=COVER,
    )
    got = exchange(send, "grp")
    send = call(
        qkv_sum_kernel, sds((N_SEQ, GROUP_ROWS, QPAD)), got, qkv_bias[None, :],
        scratch=[pltpu.VMEM((1, QPAD), F32)], cost=COVER,
    )
    got = exchange(send, "seq")
    send = call(
        attend_kernel, sds((N_SEQ, GROUP_ROWS, 4 * HEAD_DIM)),
        group_perm, lengths, page_table, got, inverse, k_pool, v_pool,
        smem=(0, 1, 2),
        scratch=[
            pltpu.VMEM((REQ_GRP, KV_HEADS * QROWS, 2 * HEAD_DIM), F32),
            pltpu.VMEM((PAGE, KV_HEADS * HEAD_DIM), BF),
            pltpu.VMEM((PAGE, KV_HEADS * HEAD_DIM), BF),
            pltpu.VMEM((KV_HEADS * QROWS, SHARD_KEYS + PAGE), F32),
            pltpu.VMEM((N_SEQ, GROUP_ROWS, 4 * HEAD_DIM), F32),
        ],
    )
    got = exchange(send, "seq")
    send = call(merge_kernel, sds((N_GRP, GROUP_ROWS, 3 * HEAD_DIM)), got)
    got = exchange(send, "grp")
    send = call(project_kernel, sds((N_SEQ, FEAT, ROWS)), got, o_weight)
    got = exchange(send, "seq")
    send, res = call(
        middle_kernel, [sds((N_SEQ, FEAT_PAD, ROWS)), sds((FEAT, ROWS), F32)],
        got, xt, gain_mid[None, :],
    )
    got = exchange(send, "seq")
    keep, give = call(
        gate_kernel,
        [sds((N_CHIP, GROUP_ROWS, 2 * FPAD), F32), sds((N_CHIP, GROUP_ROWS, 2 * FPAD))],
        got, gate_weight.T, up_weight.T,
        scratch=[pltpu.VMEM((GFEAT, ROWS), F32)],
    )
    send = call(pair_kernel, sds((N_CHIP, GROUP_ROWS, 2 * FPAD)), keep, swap_cores(give))
    got = exchange_chips(send)
    send = call(hidden_kernel, sds((N_GRP, GROUP_ROWS, FPAD)), got)
    got = exchange(send, "grp")
    send = call(project_kernel, sds((N_SEQ, FEAT, ROWS)), got, down_weight)
    got = exchange(send, "seq")
    out = call(finish_kernel, sds((ROWS, FEAT)), got, res, hot)
    return out.reshape(REQUESTS, STEPS, FEAT)


def solution(mesh):
    return jax.shard_map(
        body,
        mesh=mesh,
        in_specs=(
            P(None, None, ("grp", "seq")),
            P(),
            P(),
            P(),
            P(("grp", "seq"), None, None),
            P(("grp", "seq"), None, None),
            P(("grp", "seq")),
            P("grp", "seq"),
            P("seq"),
            P("seq", "grp"),
            P(("grp", "seq")),
            P("grp", "seq"),
            P("grp", "seq"),
            P("seq", "grp"),
        ),
        out_specs=P(None, None, ("grp", "seq")),
        check_vma=False,
    )
```

```python
import functools

import jax
import jax.numpy as jnp
import numpy as np
from jax import lax
from jax.experimental import pallas as pl
from jax.experimental.pallas import tpu as pltpu
from jax.sharding import PartitionSpec as P

D = 5120
HEADS = 40
KV_HEADS = 8
HEAD_DIM = 128
STEPS = 4
REQ_GRP = 4
SHARD_PAGES = 8
PAGE = 128
REQUESTS = 32
ROWS = REQUESTS * STEPS
GROUP_ROWS = REQ_GRP * STEPS
N_GRP = 8
N_SEQ = 16
N_CHIP = N_GRP // 2
FEAT = D // (N_GRP * N_SEQ)
FEAT_PAD = 48
GFEAT = D // N_GRP
QCOLS = 448
QPAD = 512
OCOLS = 320
FCOLS = 864
FPAD = 896
QROWS = 24
SHARD_KEYS = SHARD_PAGES * PAGE
EPSILON = 1e-06
LOW_SCORE = -1e30
ROPE_BASE = 1000000.0
BF = jnp.bfloat16
COVER = pl.CostEstimate(flops=10**10, transcendentals=0, bytes_accessed=64 << 20)
NT = (((1,), (1,)), ((), ()))
F32 = jnp.float32


def call(kernel, outs, *args, smem=(), anys=(), scratch=(), cost=None):
    specs = []
    for i in range(len(args)):
        if i in smem:
            specs.append(pl.BlockSpec(memory_space=pltpu.SMEM))
        elif i in anys:
            specs.append(pl.BlockSpec(memory_space=pltpu.HBM))
        else:
            specs.append(pl.BlockSpec(memory_space=pltpu.VMEM))
    args = [pltpu.with_memory_space_constraint(v, pltpu.HBM) if i in anys else v for i, v in enumerate(args)]
    many = isinstance(outs, (list, tuple))
    vm = pl.BlockSpec(memory_space=pltpu.VMEM)
    return pl.pallas_call(
        kernel,
        out_shape=outs,
        in_specs=specs,
        out_specs=[vm] * len(outs) if many else vm,
        scratch_shapes=list(scratch),
        name=getattr(kernel, "__name__", "kernel"),
        cost_estimate=cost,
        compiler_params=pltpu.CompilerParams(vmem_limit_bytes=16 << 20),
    )(*args)


def sds(shape, dtype=BF):
    return jax.ShapeDtypeStruct(shape, dtype)


def split(value):
    hi = value.astype(BF).astype(F32)
    return hi, value - hi


def iota(shape, axis):
    return lax.broadcasted_iota(jnp.int32, shape, axis)


def spread_features(value, squares, out_ref):
    hi, lo = split(squares)
    tail = jnp.where(iota((8, ROWS), 0) == 0, hi, jnp.where(iota((8, ROWS), 0) == 1, lo, 0.0))
    block = jnp.concatenate([value, tail], axis=0).astype(BF)
    for s in range(N_SEQ):
        out_ref[s] = block


def start_kernel(perm_hbm, tok_hbm, gain_hbm, send_ref, xt_ref, hot_ref, perm_ref, tok_ref, gain_ref, sems):
    copies = [
        pltpu.make_async_copy(perm_hbm, perm_ref, sems.at[0]),
        pltpu.make_async_copy(tok_hbm, tok_ref, sems.at[1]),
        pltpu.make_async_copy(gain_hbm, gain_ref, sems.at[2]),
    ]
    for copy in copies:
        copy.start()
    for copy in copies:
        copy.wait()
    lane = iota((8, ROWS), 1)
    source = lane & (STEPS - 1)
    for n in range(REQUESTS):
        source = source + jnp.where((lane >> 2) == n, perm_ref[n] * STEPS, 0)
    hot = jnp.where(iota((ROWS, ROWS), 0) == source[0:1, :], 1.0, 0.0).astype(BF)
    hot_ref[...] = hot
    tok = tok_ref[...]
    scaled = (tok.astype(F32) * gain_ref[...]).astype(BF)
    turn = (((0,), (0,)), ((), ()))
    xt = lax.dot_general(tok, hot, turn, preferred_element_type=F32)
    xt_ref[...] = xt
    squares = jnp.sum(xt * xt, axis=0, keepdims=True)
    spread_features(lax.dot_general(scaled, hot, turn, preferred_element_type=F32), squares, send_ref)


def collect_features(in_ref, scratch):
    squares = jnp.zeros((1, ROWS), F32)
    for s in range(N_SEQ):
        block = in_ref[s].astype(F32)
        scratch[s * FEAT : (s + 1) * FEAT, :] = block[:FEAT]
        squares = squares + block[FEAT : FEAT + 1] + block[FEAT + 1 : FEAT + 2]
    value = scratch[...].T.astype(BF)
    squares = jnp.broadcast_to(squares, (ROWS, ROWS)).T
    return value, squares


def qkv_kernel(in_ref, w_ref, out_ref, scratch):
    value, squares = collect_features(in_ref, scratch)
    part = lax.dot_general(value, w_ref[...], NT, preferred_element_type=F32)
    hi, lo = split(squares)
    for g in range(N_GRP):
        rows = slice(g * GROUP_ROWS, (g + 1) * GROUP_ROWS)
        out_ref[g, :, :QCOLS] = part[rows].astype(BF)
        out_ref[g, :, QCOLS:] = jnp.where(
            iota((GROUP_ROWS, QPAD - QCOLS), 1) < 32, hi[rows, : QPAD - QCOLS], lo[rows, : QPAD - QCOLS]
        ).astype(BF)


def scale_of(total, at):
    squares = total[:, at : at + 1] + total[:, at + 16 : at + 17]
    return lax.rsqrt(squares / D + EPSILON)


def qkv_sum_kernel(in_ref, bias_ref, out_ref, scratch):
    scratch[...] = jnp.zeros_like(scratch)
    scratch[:, :QCOLS] = bias_ref[...]
    total = in_ref[0].astype(F32)
    for g in range(1, N_GRP):
        total = total + in_ref[g].astype(F32)
    squares = total[:, QCOLS : QCOLS + 1] + total[:, QCOLS + 32 : QCOLS + 33]
    scale = lax.rsqrt(squares / D + EPSILON)
    value = total * scale + scratch[...]
    value = jnp.where(iota(value.shape, 1) < QCOLS, value, 0.0)
    odd = lax.rem(lax.axis_index("seq"), 2) == 1
    value = jnp.where(odd, pltpu.roll(value, QPAD - QCOLS, 1), value).astype(BF)
    for s in range(N_SEQ):
        out_ref[s] = value


def cos_sin(angle):
    turns = jnp.floor(angle * float(2.0 / np.pi) + 0.5)
    rest = ((angle - turns * 1.5703125) - turns * 4.837512969970703125e-4) - turns * 7.54978995489188216e-8
    square = rest * rest
    sine = ((-1.9515295891e-4 * square + 8.3321608736e-3) * square - 1.6666654611e-1) * square * rest + rest
    cosine = (
        (2.443315711809948e-5 * square - 1.388731625493765e-3) * square + 4.166664568298827e-2
    ) * square * square - 0.5 * square + 1.0
    quadrant = turns.astype(jnp.int32) & 3
    odd = (quadrant & 1) == 1
    first = jnp.where(odd, sine, cosine)
    second = jnp.where(odd, cosine, sine)
    return (
        jnp.where((quadrant == 1) | (quadrant == 2), -first, first),
        jnp.where(quadrant >= 2, -second, second),
    )


def attend_kernel(
    perm_ref, len_ref, page_ref, in_ref, inverse_ref, k_ref, v_ref, out_ref,
    qbuf, knew, vnew, sbuf, obuf,
):
    grp_idx = lax.axis_index("grp")
    seq_idx = lax.axis_index("seq")
    members = [perm_ref[grp_idx * REQ_GRP + r] for r in range(REQ_GRP)]
    row = iota((GROUP_ROWS, HEAD_DIM), 0)
    position = row & (STEPS - 1)
    for r in range(REQ_GRP):
        position = position + jnp.where((row >> 2) == r, len_ref[members[r]], 0)
    cosine, sine = cos_sin(position.astype(F32) * inverse_ref[...])
    sine = jnp.where(iota(sine.shape, 1) < HEAD_DIM // 2, -sine, sine)
    sbuf[:, :, SHARD_KEYS:] = jnp.full((2, KV_HEADS * QROWS, PAGE), LOW_SCORE, F32)
    qbuf[...] = jnp.zeros_like(qbuf)
    for pair in range(N_SEQ // 2):
        even = in_ref[2 * pair].astype(F32)
        odd = in_ref[2 * pair + 1].astype(F32)
        for k in range(7):
            lanes = slice(k * 128, (k + 1) * 128)
            olanes = slice((k - 3) * 128, (k - 2) * 128)
            if k < 3:
                value = even[:, lanes]
            elif k == 3:
                value = even[:, lanes] + odd[:, olanes]
            else:
                value = odd[:, olanes]
            head = pair * 7 + k
            if head < HEADS + KV_HEADS:
                value = value * cosine + pltpu.roll(value, HEAD_DIM // 2, 1) * sine
            if head < HEADS:
                h, j = divmod(head, HEADS // KV_HEADS)
                for r in range(REQ_GRP):
                    at = h * QROWS + j * STEPS
                    side = (h % 2) * HEAD_DIM
                    qbuf[r, at : at + STEPS, side : side + HEAD_DIM] = value[r * STEPS : (r + 1) * STEPS]
            elif head < HEADS + KV_HEADS:
                h = head - HEADS
                knew[:, h * HEAD_DIM : (h + 1) * HEAD_DIM] = value.astype(BF)
            else:
                h = head - HEADS - KV_HEADS
                vnew[:, h * HEAD_DIM : (h + 1) * HEAD_DIM] = value.astype(BF)

    score_scale = HEAD_DIM ** (-0.5)
    power = score_scale * float(np.log2(np.e))
    step = iota((2 * QROWS, GROUP_ROWS), 0) & (STEPS - 1)
    column = iota((2 * QROWS, GROUP_ROWS), 1)
    own_live = ((column & (STEPS - 1)) <= step) & (seq_idx == N_SEQ - 1)
    place = iota((8, SHARD_KEYS), 1)
    group = iota((2 * QROWS, HEAD_DIM), 1) >> 2
    word = lax.rem(group & 15, 3)
    part_lane = iota((STEPS, HEAD_DIM), 1)
    part_turn = part_lane & 63
    slots = [
        [page_ref[members[r], seq_idx * SHARD_PAGES + p] for p in range(SHARD_PAGES)] for r in range(REQ_GRP)
    ]

    def score(r, h):
        live = len_ref[members[r]] - seq_idx * SHARD_KEYS
        bias = jnp.where(place < live, 0.0, LOW_SCORE)[0:1]
        own_bias = jnp.where(own_live & ((column >> 2) == r), 0.0, LOW_SCORE)
        lanes = slice(h * HEAD_DIM, (h + 2) * HEAD_DIM)
        rows = slice(h * QROWS, (h + 2) * QROWS)
        query = qbuf[r, rows, :].astype(BF)
        keys = jnp.concatenate([k_ref[slot, :, lanes] for slot in slots[r]], axis=0)
        scores = lax.dot_general(query, keys, NT, preferred_element_type=F32)
        sbuf[r % 2, rows, :SHARD_KEYS] = scores + bias
        own = lax.dot_general(query, knew[:, lanes], NT, preferred_element_type=F32)
        sbuf[r % 2, rows, SHARD_KEYS : SHARD_KEYS + GROUP_ROWS] = own + own_bias

    for h in range(0, KV_HEADS, 2):
        score(0, h)
    for r in range(REQ_GRP):
        for pair in range(0, KV_HEADS, 2):
            if r + 1 < REQ_GRP:
                score(r + 1, pair)
            lanes = slice(pair * HEAD_DIM, (pair + 2) * HEAD_DIM)
            scores = sbuf[r % 2, pair * QROWS : (pair + 2) * QROWS, :]
            best = jnp.max(scores, axis=1, keepdims=True)
            weight = jnp.exp2((scores - best) * power)
            total = jnp.sum(weight, axis=1, keepdims=True)
            weight = weight.astype(BF)
            values = jnp.concatenate([v_ref[slot, :, lanes] for slot in slots[r]], axis=0)
            both = jnp.dot(
                weight[:, :SHARD_KEYS], values, preferred_element_type=F32
            ) + jnp.dot(
                weight[:, SHARD_KEYS : SHARD_KEYS + GROUP_ROWS], vnew[:, lanes], preferred_element_type=F32
            )
            both = both / total
            levels = jnp.where(best > 0.1 * LOW_SCORE, best * score_scale + jnp.log(total), LOW_SCORE)
            hi, rest = split(levels)
            mid, low = split(rest)
            levels = jnp.where(word == 0, hi, jnp.where(word == 1, mid, low))
            for side in range(2):
                h = pair + side
                mixed = both[side * QROWS : (side + 1) * QROWS, side * HEAD_DIM : (side + 1) * HEAD_DIM]
                level = levels[side * QROWS : (side + 1) * QROWS]
                for half in range(2):
                    to = slice(r * STEPS, (r + 1) * STEPS)
                    parts = [slice((2 * half + j) * STEPS, (2 * half + j + 1) * STEPS) for j in range(3)]
                    notes = jnp.where(
                        part_turn < 12, level[parts[0]], jnp.where(part_turn < 24, level[parts[1]], level[parts[2]])
                    )
                    spare = (2, 0)[half]
                    for j in range(3):
                        value = mixed[parts[j]]
                        if j == spare:
                            value = jnp.where((part_lane < 64) == (half == 0), value, notes)
                        obuf[2 * h + half, to, j * HEAD_DIM : (j + 1) * HEAD_DIM] = value
    for s in range(N_SEQ):
        out_ref[s] = obuf[s].astype(BF)


def merge_kernel(in_ref, out_ref):
    odd = lax.rem(lax.axis_index("seq"), 2) == 1
    levels = []
    for s in range(N_SEQ):
        first = in_ref[s, :, :HEAD_DIM].astype(F32)
        last = in_ref[s, :, 2 * HEAD_DIM :].astype(F32)
        cols = jnp.where(odd, first, pltpu.roll(last, HEAD_DIM // 2, 1))
        levels.append(
            [cols[:, a : a + 1] + cols[:, a + 4 : a + 5] + cols[:, a + 8 : a + 9] for a in (0, 12, 24)]
        )
    out = []
    for j in range(3):
        best = functools.reduce(jnp.maximum, [level[j] for level in levels])
        total = jnp.zeros_like(best)
        value = jnp.zeros((GROUP_ROWS, HEAD_DIM), F32)
        for s in range(N_SEQ):
            factor = jnp.exp(levels[s][j] - best)
            total = total + factor
            value = value + in_ref[s, :, j * HEAD_DIM : (j + 1) * HEAD_DIM].astype(F32) * factor
        out.append(value / total)
    value = jnp.concatenate(out, axis=1)
    value = jnp.where(odd, pltpu.roll(value, 3 * HEAD_DIM - HEAD_DIM // 2, 1), value).astype(BF)
    for g in range(N_GRP):
        out_ref[g] = value


def send_back(part, out_ref):
    turned = part.T
    for s in range(N_SEQ):
        out_ref[s] = turned[s * FEAT : (s + 1) * FEAT].astype(BF)


def on_second_core():
    return lax.rem(lax.axis_index("grp"), 2) == 1


def on_second_core():
    return lax.rem(lax.axis_index("grp"), 2) == 1


def project_kernel(in_ref, w_ref, out_ref):
    value = in_ref[...].reshape(ROWS, in_ref.shape[2])[:, : w_ref.shape[0]]
    send_back(jnp.dot(value, w_ref[...], preferred_element_type=F32), out_ref)


def middle_kernel(in_ref, xt_ref, gain_ref, send_ref, res_ref):
    total = xt_ref[...]
    part = in_ref[0].astype(F32)
    for s in range(1, N_SEQ):
        part = part + in_ref[s].astype(F32)
    total = total + part
    res_ref[...] = total
    squares = jnp.sum(total * total, axis=0, keepdims=True)
    diagonal = iota((FEAT, FEAT), 0) == iota((FEAT, FEAT), 1)
    gain = jnp.sum(jnp.where(diagonal, gain_ref[...], 0.0), axis=1, keepdims=True)
    spread_features(total * gain, squares, send_ref)


def gate_kernel(in_ref, gate_ref, up_ref, keep_ref, give_ref, scratch):
    value, squares = collect_features(in_ref, scratch)
    gate = lax.dot_general(value, gate_ref[...], NT, preferred_element_type=F32)
    up = lax.dot_general(value, up_ref[...], NT, preferred_element_type=F32)
    hi, lo = split(squares)
    tail = FPAD - FCOLS
    sums = jnp.where(iota((ROWS, tail), 1) < tail // 2, hi[:, :tail], lo[:, :tail])
    second = on_second_core()
    spare = slice(FCOLS, FPAD)
    for x in range(N_CHIP):
        first_rows = slice(2 * x * GROUP_ROWS, (2 * x + 1) * GROUP_ROWS)
        last_rows = slice((2 * x + 1) * GROUP_ROWS, (2 * x + 2) * GROUP_ROWS)
        for lanes, part in (
            (slice(0, FCOLS), gate),
            (spare, sums),
            (slice(FPAD, FPAD + FCOLS), up),
        ):
            first = part[first_rows]
            last = part[last_rows]
            keep_ref[x, :, lanes] = jnp.where(second, last, first)
            give_ref[x, :, lanes] = jnp.where(second, first, last).astype(BF)
        keep_ref[x, :, FPAD + FCOLS :] = jnp.zeros((GROUP_ROWS, tail), F32)
        give_ref[x, :, FPAD + FCOLS :] = jnp.zeros((GROUP_ROWS, tail), BF)


def pair_kernel(keep_ref, got_ref, out_ref):
    tail = (FPAD - FCOLS) // 2
    start = FPAD - 128
    lane = iota((GROUP_ROWS, 128), 1)
    for x in range(N_CHIP):
        total = keep_ref[x] + got_ref[x].astype(F32)
        out_ref[x] = total.astype(BF)
        last = total[:, start:FPAD]
        hi, lo = split(last + pltpu.roll(last, 128 - tail, 1))
        last = jnp.where(
            lane < 128 - 2 * tail, last, jnp.where(lane < 128 - tail, hi, pltpu.roll(lo, tail, 1))
        )
        out_ref[x, :, start:FPAD] = last.astype(BF)


def hidden_kernel(in_ref, out_ref):
    total = in_ref[0].astype(F32)
    for x in range(1, N_CHIP):
        total = total + in_ref[x].astype(F32)
    scale = scale_of(total, FCOLS)
    gate = total[:, :FPAD] * scale
    up = total[:, FPAD:] * scale
    value = (gate / (1.0 + jnp.exp(-gate)) * up).astype(BF)
    for g in range(N_GRP):
        out_ref[g] = value


def finish_kernel(in_ref, res_ref, hot_ref, out_ref):
    part = in_ref[0].astype(F32)
    for s in range(1, N_SEQ):
        part = part + in_ref[s].astype(F32)
    total = (res_ref[...] + part).astype(BF)
    out_ref[...] = lax.dot_general(
        hot_ref[...], total, (((1,), (1,)), ((), ())), preferred_element_type=F32
    ).astype(BF)


def exchange(value, axis):
    return lax.all_to_all(value, axis, 0, 0, tiled=False)


def exchange_chips(value):
    groups = [list(range(core, N_GRP, 2)) for core in range(2)]
    return lax.all_to_all(value, "grp", 0, 0, axis_index_groups=groups, tiled=False)


def swap_cores(value):
    return lax.ppermute(value, "grp", [(i, i ^ 1) for i in range(N_GRP)])


def body(
    tokens, lengths, group_perm, page_table, k_pool, v_pool, gain_in, qkv_weight, qkv_bias,
    o_weight, gain_mid, gate_weight, up_weight, down_weight,
):
    half = HEAD_DIM // 2
    inverse = np.exp(-np.arange(half) * (2.0 / HEAD_DIM) * np.log(ROPE_BASE)).astype(np.float32)
    inverse = jnp.asarray(np.concatenate([inverse, inverse]))[None, :]

    send, xt, hot = call(
        start_kernel,
        [sds((N_SEQ, FEAT_PAD, ROWS)), sds((FEAT, ROWS), F32), sds((ROWS, ROWS))],
        group_perm, tokens.reshape(ROWS, FEAT), gain_in[None, :],
        anys=(0, 1, 2),
        scratch=[
            pltpu.SMEM((REQUESTS,), jnp.int32),
            pltpu.VMEM((ROWS, FEAT), BF),
            pltpu.VMEM((1, FEAT), F32),
            pltpu.SemaphoreType.DMA((3,)),
        ],
        cost=COVER,
    )
    got = exchange(send, "seq")
    send = call(
        qkv_kernel, sds((N_GRP, GROUP_ROWS, QPAD)), got, qkv_weight.T,
        scratch=[pltpu.VMEM((GFEAT, ROWS), F32)], cost=COVER,
    )
    got = exchange(send, "grp")
    send = call(
        qkv_sum_kernel, sds((N_SEQ, GROUP_ROWS, QPAD)), got, qkv_bias[None, :],
        scratch=[pltpu.VMEM((1, QPAD), F32)], cost=COVER,
    )
    got = exchange(send, "seq")
    send = call(
        attend_kernel, sds((N_SEQ, GROUP_ROWS, 3 * HEAD_DIM)),
        group_perm, lengths, page_table, got, inverse, k_pool, v_pool,
        smem=(0, 1, 2),
        scratch=[
            pltpu.VMEM((REQ_GRP, KV_HEADS * QROWS, 2 * HEAD_DIM), F32),
            pltpu.VMEM((GROUP_ROWS, KV_HEADS * HEAD_DIM), BF),
            pltpu.VMEM((GROUP_ROWS, KV_HEADS * HEAD_DIM), BF),
            pltpu.VMEM((2, KV_HEADS * QROWS, SHARD_KEYS + PAGE), F32),
            pltpu.VMEM((N_SEQ, GROUP_ROWS, 3 * HEAD_DIM), F32),
        ],
    )
    got = exchange(send, "seq")
    send = call(merge_kernel, sds((N_GRP, GROUP_ROWS, 3 * HEAD_DIM)), got)
    got = exchange(send, "grp")
    send = call(project_kernel, sds((N_SEQ, FEAT, ROWS)), got, o_weight)
    got = exchange(send, "seq")
    send, res = call(
        middle_kernel, [sds((N_SEQ, FEAT_PAD, ROWS)), sds((FEAT, ROWS), F32)],
        got, xt, gain_mid[None, :],
    )
    got = exchange(send, "seq")
    keep, give = call(
        gate_kernel,
        [sds((N_CHIP, GROUP_ROWS, 2 * FPAD), F32), sds((N_CHIP, GROUP_ROWS, 2 * FPAD))],
        got, gate_weight.T, up_weight.T,
        scratch=[pltpu.VMEM((GFEAT, ROWS), F32)],
    )
    send = call(pair_kernel, sds((N_CHIP, GROUP_ROWS, 2 * FPAD)), keep, swap_cores(give))
    got = exchange_chips(send)
    send = call(hidden_kernel, sds((N_GRP, GROUP_ROWS, FPAD)), got)
    got = exchange(send, "grp")
    send = call(project_kernel, sds((N_SEQ, FEAT, ROWS)), got, down_weight)
    got = exchange(send, "seq")
    out = call(finish_kernel, sds((ROWS, FEAT)), got, res, hot)
    return out.reshape(REQUESTS, STEPS, FEAT)


def solution(mesh):
    return jax.shard_map(
        body,
        mesh=mesh,
        in_specs=(
            P(None, None, ("grp", "seq")),
            P(),
            P(),
            P(),
            P(("grp", "seq"), None, None),
            P(("grp", "seq"), None, None),
            P(("grp", "seq")),
            P("grp", "seq"),
            P("seq"),
            P("seq", "grp"),
            P(("grp", "seq")),
            P("grp", "seq"),
            P("grp", "seq"),
            P("seq", "grp"),
        ),
        out_specs=P(None, None, ("grp", "seq")),
        check_vma=False,
    )
```

```python
import functools

import jax
import jax.numpy as jnp
import numpy as np
from jax import lax
from jax.experimental import pallas as pl
from jax.experimental.pallas import tpu as pltpu
from jax.sharding import PartitionSpec as P

D = 5120
HEADS = 40
KV_HEADS = 8
HEAD_DIM = 128
STEPS = 4
REQ_GRP = 4
SHARD_PAGES = 8
PAGE = 128
REQUESTS = 32
ROWS = REQUESTS * STEPS
GROUP_ROWS = REQ_GRP * STEPS
N_GRP = 8
N_SEQ = 16
N_CHIP = N_GRP // 2
FEAT = D // (N_GRP * N_SEQ)
FEAT_PAD = 48
GFEAT = D // N_GRP
QCOLS = 448
QPAD = 512
OCOLS = 320
FCOLS = 864
FPAD = 896
QROWS = 24
SHARD_KEYS = SHARD_PAGES * PAGE
EPSILON = 1e-06
LOW_SCORE = -1e30
ROPE_BASE = 1000000.0
BF = jnp.bfloat16
COVER = pl.CostEstimate(flops=10**10, transcendentals=0, bytes_accessed=64 << 20)
NT = (((1,), (1,)), ((), ()))
F32 = jnp.float32


def call(kernel, outs, *args, smem=(), anys=(), scratch=(), cost=None):
    specs = []
    for i in range(len(args)):
        if i in smem:
            specs.append(pl.BlockSpec(memory_space=pltpu.SMEM))
        elif i in anys:
            specs.append(pl.BlockSpec(memory_space=pltpu.HBM))
        else:
            specs.append(pl.BlockSpec(memory_space=pltpu.VMEM))
    args = [pltpu.with_memory_space_constraint(v, pltpu.HBM) if i in anys else v for i, v in enumerate(args)]
    many = isinstance(outs, (list, tuple))
    vm = pl.BlockSpec(memory_space=pltpu.VMEM)
    return pl.pallas_call(
        kernel,
        out_shape=outs,
        in_specs=specs,
        out_specs=[vm] * len(outs) if many else vm,
        scratch_shapes=list(scratch),
        name=getattr(kernel, "__name__", "kernel"),
        cost_estimate=cost,
        compiler_params=pltpu.CompilerParams(vmem_limit_bytes=16 << 20),
    )(*args)


def sds(shape, dtype=BF):
    return jax.ShapeDtypeStruct(shape, dtype)


def split(value):
    hi = value.astype(BF).astype(F32)
    return hi, value - hi


def iota(shape, axis):
    return lax.broadcasted_iota(jnp.int32, shape, axis)


def spread_features(value, squares, out_ref):
    hi, lo = split(squares)
    tail = jnp.where(iota((8, ROWS), 0) == 0, hi, jnp.where(iota((8, ROWS), 0) == 1, lo, 0.0))
    block = jnp.concatenate([value, tail], axis=0).astype(BF)
    for s in range(N_SEQ):
        out_ref[s] = block


def start_kernel(perm_hbm, tok_hbm, gain_hbm, send_ref, xt_ref, hot_ref, perm_ref, tok_ref, gain_ref, sems):
    copies = [
        pltpu.make_async_copy(perm_hbm, perm_ref, sems.at[0]),
        pltpu.make_async_copy(tok_hbm, tok_ref, sems.at[1]),
        pltpu.make_async_copy(gain_hbm, gain_ref, sems.at[2]),
    ]
    for copy in copies:
        copy.start()
    for copy in copies:
        copy.wait()
    lane = iota((8, ROWS), 1)
    source = lane & (STEPS - 1)
    for n in range(REQUESTS):
        source = source + jnp.where((lane >> 2) == n, perm_ref[n] * STEPS, 0)
    hot = jnp.where(iota((ROWS, ROWS), 0) == source[0:1, :], 1.0, 0.0).astype(BF)
    hot_ref[...] = hot
    tok = tok_ref[...]
    scaled = (tok.astype(F32) * gain_ref[...]).astype(BF)
    turn = (((0,), (0,)), ((), ()))
    xt = lax.dot_general(tok, hot, turn, preferred_element_type=F32)
    xt_ref[...] = xt
    squares = jnp.sum(xt * xt, axis=0, keepdims=True)
    spread_features(lax.dot_general(scaled, hot, turn, preferred_element_type=F32), squares, send_ref)


def collect_features(in_ref, scratch):
    squares = jnp.zeros((1, ROWS), F32)
    for s in range(N_SEQ):
        block = in_ref[s].astype(F32)
        scratch[s * FEAT : (s + 1) * FEAT, :] = block[:FEAT]
        squares = squares + block[FEAT : FEAT + 1] + block[FEAT + 1 : FEAT + 2]
    value = scratch[...].T.astype(BF)
    squares = jnp.broadcast_to(squares, (ROWS, ROWS)).T
    return value, squares


def qkv_kernel(in_ref, w_ref, out_ref, scratch):
    value, squares = collect_features(in_ref, scratch)
    part = lax.dot_general(value, w_ref[...], NT, preferred_element_type=F32)
    hi, lo = split(squares)
    for g in range(N_GRP):
        rows = slice(g * GROUP_ROWS, (g + 1) * GROUP_ROWS)
        out_ref[g, :, :QCOLS] = part[rows].astype(BF)
        out_ref[g, :, QCOLS:] = jnp.where(
            iota((GROUP_ROWS, QPAD - QCOLS), 1) < 32, hi[rows, : QPAD - QCOLS], lo[rows, : QPAD - QCOLS]
        ).astype(BF)


def scale_of(total, at):
    squares = total[:, at : at + 1] + total[:, at + 16 : at + 17]
    return lax.rsqrt(squares / D + EPSILON)


def qkv_sum_kernel(in_ref, bias_ref, out_ref, scratch):
    scratch[...] = jnp.zeros_like(scratch)
    scratch[:, :QCOLS] = bias_ref[...]
    total = in_ref[0].astype(F32)
    for g in range(1, N_GRP):
        total = total + in_ref[g].astype(F32)
    squares = total[:, QCOLS : QCOLS + 1] + total[:, QCOLS + 32 : QCOLS + 33]
    scale = lax.rsqrt(squares / D + EPSILON)
    value = total * scale + scratch[...]
    value = jnp.where(iota(value.shape, 1) < QCOLS, value, 0.0)
    odd = lax.rem(lax.axis_index("seq"), 2) == 1
    value = jnp.where(odd, pltpu.roll(value, QPAD - QCOLS, 1), value).astype(BF)
    for s in range(N_SEQ):
        out_ref[s] = value


def cos_sin(angle):
    turns = jnp.floor(angle * float(2.0 / np.pi) + 0.5)
    rest = ((angle - turns * 1.5703125) - turns * 4.837512969970703125e-4) - turns * 7.54978995489188216e-8
    square = rest * rest
    sine = ((-1.9515295891e-4 * square + 8.3321608736e-3) * square - 1.6666654611e-1) * square * rest + rest
    cosine = (
        (2.443315711809948e-5 * square - 1.388731625493765e-3) * square + 4.166664568298827e-2
    ) * square * square - 0.5 * square + 1.0
    quadrant = turns.astype(jnp.int32) & 3
    odd = (quadrant & 1) == 1
    first = jnp.where(odd, sine, cosine)
    second = jnp.where(odd, cosine, sine)
    return (
        jnp.where((quadrant == 1) | (quadrant == 2), -first, first),
        jnp.where(quadrant >= 2, -second, second),
    )


def attend_kernel(
    perm_ref, len_ref, page_ref, in_ref, inverse_ref, k_ref, v_ref, out_ref,
    qbuf, knew, vnew, sbuf, obuf,
):
    grp_idx = lax.axis_index("grp")
    seq_idx = lax.axis_index("seq")
    members = [perm_ref[grp_idx * REQ_GRP + r] for r in range(REQ_GRP)]
    row = iota((GROUP_ROWS, HEAD_DIM), 0)
    position = row & (STEPS - 1)
    for r in range(REQ_GRP):
        position = position + jnp.where((row >> 2) == r, len_ref[members[r]], 0)
    cosine, sine = cos_sin(position.astype(F32) * inverse_ref[...])
    sine = jnp.where(iota(sine.shape, 1) < HEAD_DIM // 2, -sine, sine)
    sbuf[:, :, SHARD_KEYS:] = jnp.full((2, KV_HEADS * QROWS, PAGE), LOW_SCORE, F32)
    qbuf[...] = jnp.zeros_like(qbuf)
    for pair in range(N_SEQ // 2):
        even = in_ref[2 * pair].astype(F32)
        odd = in_ref[2 * pair + 1].astype(F32)
        for k in range(7):
            lanes = slice(k * 128, (k + 1) * 128)
            olanes = slice((k - 3) * 128, (k - 2) * 128)
            if k < 3:
                value = even[:, lanes]
            elif k == 3:
                value = even[:, lanes] + odd[:, olanes]
            else:
                value = odd[:, olanes]
            head = pair * 7 + k
            if head < HEADS + KV_HEADS:
                value = value * cosine + pltpu.roll(value, HEAD_DIM // 2, 1) * sine
            if head < HEADS:
                h, j = divmod(head, HEADS // KV_HEADS)
                for r in range(REQ_GRP):
                    at = h * QROWS + j * STEPS
                    side = (h % 2) * HEAD_DIM
                    qbuf[r, at : at + STEPS, side : side + HEAD_DIM] = value[r * STEPS : (r + 1) * STEPS]
            elif head < HEADS + KV_HEADS:
                h = head - HEADS
                knew[:, h * HEAD_DIM : (h + 1) * HEAD_DIM] = value.astype(BF)
            else:
                h = head - HEADS - KV_HEADS
                vnew[:, h * HEAD_DIM : (h + 1) * HEAD_DIM] = value.astype(BF)

    score_scale = HEAD_DIM ** (-0.5)
    power = score_scale * float(np.log2(np.e))
    step = iota((2 * QROWS, GROUP_ROWS), 0) & (STEPS - 1)
    column = iota((2 * QROWS, GROUP_ROWS), 1)
    own_live = ((column & (STEPS - 1)) <= step) & (seq_idx == N_SEQ - 1)
    place = iota((8, SHARD_KEYS), 1)
    group = iota((2 * QROWS, HEAD_DIM), 1) >> 2
    word = lax.rem(group & 15, 3)
    part_lane = iota((STEPS, HEAD_DIM), 1)
    part_turn = part_lane & 63
    slots = [
        [page_ref[members[r], seq_idx * SHARD_PAGES + p] for p in range(SHARD_PAGES)] for r in range(REQ_GRP)
    ]

    def score(r, h):
        live = len_ref[members[r]] - seq_idx * SHARD_KEYS
        bias = jnp.where(place < live, 0.0, LOW_SCORE)[0:1]
        own_bias = jnp.where(own_live & ((column >> 2) == r), 0.0, LOW_SCORE)
        lanes = slice(h * HEAD_DIM, (h + 2) * HEAD_DIM)
        rows = slice(h * QROWS, (h + 2) * QROWS)
        query = qbuf[r, rows, :].astype(BF)
        keys = jnp.concatenate([k_ref[slot, :, lanes] for slot in slots[r]], axis=0)
        scores = lax.dot_general(query, keys, NT, preferred_element_type=F32)
        sbuf[r % 2, rows, :SHARD_KEYS] = scores + bias
        own = lax.dot_general(query, knew[:, lanes], NT, preferred_element_type=F32)
        sbuf[r % 2, rows, SHARD_KEYS : SHARD_KEYS + GROUP_ROWS] = own + own_bias

    for h in range(0, KV_HEADS, 2):
        score(0, h)
    for r in range(REQ_GRP):
        for pair in range(0, KV_HEADS, 2):
            if r + 1 < REQ_GRP:
                score(r + 1, pair)
            lanes = slice(pair * HEAD_DIM, (pair + 2) * HEAD_DIM)
            scores = sbuf[r % 2, pair * QROWS : (pair + 2) * QROWS, :]
            best = jnp.max(scores, axis=1, keepdims=True)
            weight = jnp.exp2((scores - best) * power)
            total = jnp.sum(weight, axis=1, keepdims=True)
            weight = weight.astype(BF)
            values = jnp.concatenate([v_ref[slot, :, lanes] for slot in slots[r]], axis=0)
            both = jnp.dot(
                weight[:, :SHARD_KEYS], values, preferred_element_type=F32
            ) + jnp.dot(
                weight[:, SHARD_KEYS : SHARD_KEYS + GROUP_ROWS], vnew[:, lanes], preferred_element_type=F32
            )
            both = both / total
            levels = jnp.where(best > 0.1 * LOW_SCORE, best * score_scale + jnp.log(total), LOW_SCORE)
            hi, rest = split(levels)
            mid, low = split(rest)
            levels = jnp.where(word == 0, hi, jnp.where(word == 1, mid, low))
            for side in range(2):
                h = pair + side
                mixed = both[side * QROWS : (side + 1) * QROWS, side * HEAD_DIM : (side + 1) * HEAD_DIM]
                level = levels[side * QROWS : (side + 1) * QROWS]
                for half in range(2):
                    to = slice(r * STEPS, (r + 1) * STEPS)
                    parts = [slice((2 * half + j) * STEPS, (2 * half + j + 1) * STEPS) for j in range(3)]
                    notes = jnp.where(
                        part_turn < 12, level[parts[0]], jnp.where(part_turn < 24, level[parts[1]], level[parts[2]])
                    )
                    spare = (2, 0)[half]
                    for j in range(3):
                        value = mixed[parts[j]]
                        if j == spare:
                            value = jnp.where((part_lane < 64) == (half == 0), value, notes)
                        obuf[2 * h + half, to, j * HEAD_DIM : (j + 1) * HEAD_DIM] = value
    for s in range(N_SEQ):
        out_ref[s] = obuf[s].astype(BF)


def merge_kernel(in_ref, out_ref):
    odd = lax.rem(lax.axis_index("seq"), 2) == 1
    levels = []
    for s in range(N_SEQ):
        first = in_ref[s, :, :HEAD_DIM].astype(F32)
        last = in_ref[s, :, 2 * HEAD_DIM :].astype(F32)
        cols = jnp.where(odd, first, pltpu.roll(last, HEAD_DIM // 2, 1))
        levels.append(
            [cols[:, a : a + 1] + cols[:, a + 4 : a + 5] + cols[:, a + 8 : a + 9] for a in (0, 12, 24)]
        )
    out = []
    for j in range(3):
        best = functools.reduce(jnp.maximum, [level[j] for level in levels])
        total = jnp.zeros_like(best)
        value = jnp.zeros((GROUP_ROWS, HEAD_DIM), F32)
        for s in range(N_SEQ):
            factor = jnp.exp(levels[s][j] - best)
            total = total + factor
            value = value + in_ref[s, :, j * HEAD_DIM : (j + 1) * HEAD_DIM].astype(F32) * factor
        out.append(value / total)
    value = jnp.concatenate(out, axis=1)
    value = jnp.where(odd, pltpu.roll(value, 3 * HEAD_DIM - HEAD_DIM // 2, 1), value).astype(BF)
    for g in range(N_GRP):
        out_ref[g] = value


def send_back(part, out_ref):
    turned = part.T
    for s in range(N_SEQ):
        out_ref[s] = turned[s * FEAT : (s + 1) * FEAT].astype(BF)


def on_second_core():
    return lax.rem(lax.axis_index("grp"), 2) == 1


def on_second_core():
    return lax.rem(lax.axis_index("grp"), 2) == 1


def project_kernel(in_ref, w_ref, out_ref):
    value = in_ref[...].reshape(ROWS, in_ref.shape[2])[:, : w_ref.shape[0]]
    send_back(jnp.dot(value, w_ref[...], preferred_element_type=F32), out_ref)


def middle_kernel(in_ref, xt_ref, gain_ref, send_ref, res_ref):
    total = xt_ref[...]
    part = in_ref[0].astype(F32)
    for s in range(1, N_SEQ):
        part = part + in_ref[s].astype(F32)
    total = total + part
    res_ref[...] = total
    squares = jnp.sum(total * total, axis=0, keepdims=True)
    diagonal = iota((FEAT, FEAT), 0) == iota((FEAT, FEAT), 1)
    gain = jnp.sum(jnp.where(diagonal, gain_ref[...], 0.0), axis=1, keepdims=True)
    spread_features(total * gain, squares, send_ref)


def half_kernel(kept, in_ref, gate_ref, up_ref, out_ref, scratch):
    value, squares = collect_features(in_ref, scratch)
    second = on_second_core()

    def by_core(rows):
        blocks = [rows[g * GROUP_ROWS : (g + 1) * GROUP_ROWS] for g in range(N_GRP)]
        pairs = list(zip(blocks[0::2], blocks[1::2]))
        if kept:
            return jnp.concatenate([jnp.where(second, last, first) for first, last in pairs], axis=0)
        return jnp.concatenate([jnp.where(second, first, last) for first, last in pairs], axis=0)

    value = by_core(value)
    gate = lax.dot_general(value, gate_ref[...], NT, preferred_element_type=F32)
    up = lax.dot_general(value, up_ref[...], NT, preferred_element_type=F32)
    hi, lo = split(squares)
    tail = FPAD - FCOLS
    sums = by_core(jnp.where(iota((ROWS, tail), 1) < tail // 2, hi[:, :tail], lo[:, :tail]))
    for x in range(N_CHIP):
        rows = slice(x * GROUP_ROWS, (x + 1) * GROUP_ROWS)
        for start, part in ((0, gate), (FCOLS, sums), (FPAD, up)):
            out_ref[x, :, start : start + part.shape[1]] = part[rows].astype(out_ref.dtype)
        out_ref[x, :, FPAD + FCOLS :] = jnp.zeros((GROUP_ROWS, tail), out_ref.dtype)


def give_kernel(*refs):
    half_kernel(False, *refs)


def keep_kernel(*refs):
    half_kernel(True, *refs)


def pair_kernel(keep_ref, got_ref, out_ref):
    tail = (FPAD - FCOLS) // 2
    start = FPAD - 128
    lane = iota((GROUP_ROWS, 128), 1)
    for x in range(N_CHIP):
        total = keep_ref[x] + got_ref[x].astype(F32)
        out_ref[x] = total.astype(BF)
        last = total[:, start:FPAD]
        hi, lo = split(last + pltpu.roll(last, 128 - tail, 1))
        last = jnp.where(
            lane < 128 - 2 * tail, last, jnp.where(lane < 128 - tail, hi, pltpu.roll(lo, tail, 1))
        )
        out_ref[x, :, start:FPAD] = last.astype(BF)


def hidden_kernel(in_ref, out_ref):
    total = in_ref[0].astype(F32)
    for x in range(1, N_CHIP):
        total = total + in_ref[x].astype(F32)
    scale = scale_of(total, FCOLS)
    gate = total[:, :FPAD] * scale
    up = total[:, FPAD:] * scale
    value = (gate / (1.0 + jnp.exp(-gate)) * up).astype(BF)
    for g in range(N_GRP):
        out_ref[g] = value


def finish_kernel(in_ref, res_ref, hot_ref, out_ref):
    part = in_ref[0].astype(F32)
    for s in range(1, N_SEQ):
        part = part + in_ref[s].astype(F32)
    total = (res_ref[...] + part).astype(BF)
    out_ref[...] = lax.dot_general(
        hot_ref[...], total, (((1,), (1,)), ((), ())), preferred_element_type=F32
    ).astype(BF)


def exchange(value, axis):
    return lax.all_to_all(value, axis, 0, 0, tiled=False)


def exchange_chips(value):
    groups = [list(range(core, N_GRP, 2)) for core in range(2)]
    return lax.all_to_all(value, "grp", 0, 0, axis_index_groups=groups, tiled=False)


def swap_cores(value):
    return lax.ppermute(value, "grp", [(i, i ^ 1) for i in range(N_GRP)])


def body(
    tokens, lengths, group_perm, page_table, k_pool, v_pool, gain_in, qkv_weight, qkv_bias,
    o_weight, gain_mid, gate_weight, up_weight, down_weight,
):
    half = HEAD_DIM // 2
    inverse = np.exp(-np.arange(half) * (2.0 / HEAD_DIM) * np.log(ROPE_BASE)).astype(np.float32)
    inverse = jnp.asarray(np.concatenate([inverse, inverse]))[None, :]

    send, xt, hot = call(
        start_kernel,
        [sds((N_SEQ, FEAT_PAD, ROWS)), sds((FEAT, ROWS), F32), sds((ROWS, ROWS))],
        group_perm, tokens.reshape(ROWS, FEAT), gain_in[None, :],
        anys=(0, 1, 2),
        scratch=[
            pltpu.SMEM((REQUESTS,), jnp.int32),
            pltpu.VMEM((ROWS, FEAT), BF),
            pltpu.VMEM((1, FEAT), F32),
            pltpu.SemaphoreType.DMA((3,)),
        ],
        cost=COVER,
    )
    got = exchange(send, "seq")
    send = call(
        qkv_kernel, sds((N_GRP, GROUP_ROWS, QPAD)), got, qkv_weight.T,
        scratch=[pltpu.VMEM((GFEAT, ROWS), F32)], cost=COVER,
    )
    got = exchange(send, "grp")
    send = call(
        qkv_sum_kernel, sds((N_SEQ, GROUP_ROWS, QPAD)), got, qkv_bias[None, :],
        scratch=[pltpu.VMEM((1, QPAD), F32)], cost=COVER,
    )
    got = exchange(send, "seq")
    send = call(
        attend_kernel, sds((N_SEQ, GROUP_ROWS, 3 * HEAD_DIM)),
        group_perm, lengths, page_table, got, inverse, k_pool, v_pool,
        smem=(0, 1, 2),
        scratch=[
            pltpu.VMEM((REQ_GRP, KV_HEADS * QROWS, 2 * HEAD_DIM), F32),
            pltpu.VMEM((GROUP_ROWS, KV_HEADS * HEAD_DIM), BF),
            pltpu.VMEM((GROUP_ROWS, KV_HEADS * HEAD_DIM), BF),
            pltpu.VMEM((2, KV_HEADS * QROWS, SHARD_KEYS + PAGE), F32),
            pltpu.VMEM((N_SEQ, GROUP_ROWS, 3 * HEAD_DIM), F32),
        ],
    )
    got = exchange(send, "seq")
    send = call(merge_kernel, sds((N_GRP, GROUP_ROWS, 3 * HEAD_DIM)), got)
    got = exchange(send, "grp")
    send = call(project_kernel, sds((N_SEQ, FEAT, ROWS)), got, o_weight)
    got = exchange(send, "seq")
    send, res = call(
        middle_kernel, [sds((N_SEQ, FEAT_PAD, ROWS)), sds((FEAT, ROWS), F32)],
        got, xt, gain_mid[None, :],
    )
    got = exchange(send, "seq")
    halves = (got, gate_weight.T, up_weight.T)
    room = [pltpu.VMEM((GFEAT, ROWS), F32)]
    shape = (N_CHIP, GROUP_ROWS, 2 * FPAD)
    other = swap_cores(call(give_kernel, sds(shape), *halves, scratch=room))
    keep = call(keep_kernel, sds(shape, F32), *halves, scratch=room, cost=COVER)
    send = call(pair_kernel, sds(shape), keep, other)
    got = exchange_chips(send)
    send = call(hidden_kernel, sds((N_GRP, GROUP_ROWS, FPAD)), got)
    got = exchange(send, "grp")
    send = call(project_kernel, sds((N_SEQ, FEAT, ROWS)), got, down_weight)
    got = exchange(send, "seq")
    out = call(finish_kernel, sds((ROWS, FEAT)), got, res, hot)
    return out.reshape(REQUESTS, STEPS, FEAT)


def solution(mesh):
    return jax.shard_map(
        body,
        mesh=mesh,
        in_specs=(
            P(None, None, ("grp", "seq")),
            P(),
            P(),
            P(),
            P(("grp", "seq"), None, None),
            P(("grp", "seq"), None, None),
            P(("grp", "seq")),
            P("grp", "seq"),
            P("seq"),
            P("seq", "grp"),
            P(("grp", "seq")),
            P("grp", "seq"),
            P("grp", "seq"),
            P("seq", "grp"),
        ),
        out_specs=P(None, None, ("grp", "seq")),
        check_vma=False,
    )
```
